1024 devices in a mesh: curve: 128 (over x, z), group: 8 (over y, core).
Axes of the slice: x: 4, y: 4, z: 32, core: 2. Of those that a mesh axis runs over, the one named last changes fastest.
Arguments:
- positions: float32 [8, 2048, 3, 128], P('group', 'curve'), may hold values from 0 to 77.2, as said below
- velocities: float32 [8, 2048, 3, 128], P('group', 'curve'), may hold values from -3 to 3
- masses: float32 [8, 2048, 128], P('group', 'curve'), may hold values from 0.003 to 0.03
- counts: int32 [8, 2048], P('group', 'curve'), may hold values from 64 to 128
- neighbours_first: int32 [8, 2048, 6], P('group', 'curve'), may hold values from 0 to 23, as said below
- sends_first: int32 [8, 1024], P('group', 'curve'), may hold values from 0 to 15, as said below
- new_slot: int32 [8, 2048], P('group', 'curve'), may hold values from 0 to 127, as said below
- neighbours_second: int32 [8, 2048, 6], P('group', 'curve'), may hold values from 0 to 23, as said below
- sends_second: int32 [8, 1024], P('group', 'curve'), may hold values from 0 to 15, as said below
Outputs:
- positions_out: float32 [8, 2048, 3, 128], P('group', 'curve')
- velocities_out: float32 [8, 2048, 3, 128], P('group', 'curve')
- densities_out: float32 [8, 2048, 128], P('group', 'curve')
The draws below stay inside these ranges and needn't reach their ends.
Inputs may be any that keep to these rules, and one draw needn't show every extreme that they name: `positions`: the particles of blocks c * 16 to c * 16 + 15 of every group have first component in [0.6 c, 0.6 c + 1) and other components in [0, 1). `neighbours_first`: A block's list holds 6 distinct candidate numbers, never the block's own slot. `neighbours_second`: A block's list holds 6 distinct candidate numbers, never the block's own slot. `sends_first`: each of a device's two lists of 4 holds distinct slots. `sends_second`: each of a device's two lists of 4 holds distinct slots. For each curve segment, new_slot over all groups' blocks of that segment is a permutation; from one device at most 2 blocks go to any one other group, and in every segment some device sends exactly 2 to some other group.
All inputs are finite; a program needn't handle non-finite values.
Results may differ from the reference program's by a relative error of at most 0.0003.
Values sent between devices are 32-bit elements; how exact they have to be, the bound alone decides.
No kernel may reach another device: no remote copies, remote signals or barrier semaphores. Data moves between devices by JAX's collectives and lax.ppermute only.
A program may use at most 32 MiB of HBM per device.

```python
import math
import jax
import jax.numpy as jnp
from jax import lax

P_SIZE = 128
BLK_DEV = 16
NBR = 6
HALO = 4
MOVE_CAP = 2
NBLK = 2048
N_CURVE = 128
N_GROUP = 8


def draw_positions(key, part):
    key_corner, key_inner = jax.random.split(jax.random.fold_in(key, 41))
    corner = 0.4 * jax.random.uniform(key_corner, (N_GROUP, NBLK, 3, 1), jnp.float32)
    inner = jax.random.uniform(key_inner, (N_GROUP, NBLK, 3, P_SIZE), jnp.float32)
    inner = 0.6 * jnp.minimum(inner, 0.999)
    segment = (jnp.arange(NBLK, dtype=jnp.int32) // BLK_DEV).astype(jnp.float32)
    first_axis = (jnp.arange(3, dtype=jnp.int32) == 0).astype(jnp.float32)
    base = 0.6 * segment[None, :, None, None] * first_axis[None, None, :, None]
    return (base + corner + inner).astype(jnp.float32)


def neighbour_draw(key):
    choices_all = BLK_DEV + 2 * HALO
    scores = jax.random.randint(key, (N_GROUP, NBLK, choices_all), 0, 1 << 20) * choices_all
    scores = scores + jnp.arange(choices_all, dtype=jnp.int32)[None, None, :]
    own = (jnp.arange(NBLK, dtype=jnp.int32) % BLK_DEV)[None, :, None] == jnp.arange(choices_all, dtype=jnp.int32)[None, None, :]
    scores = jnp.where(own, (1 << 20) * choices_all + choices_all, scores)
    order = jnp.argsort(scores, axis=-1)[..., :NBR]
    return order.astype(jnp.int32)


def send_draw(key):
    scores = jax.random.randint(key, (N_GROUP, N_CURVE, 2, BLK_DEV), 0, 1 << 20) * BLK_DEV
    scores = scores + jnp.arange(BLK_DEV, dtype=jnp.int32)
    order = jnp.argsort(scores, axis=-1)[..., :HALO]
    return order.reshape(N_GROUP, N_CURVE * 2 * HALO).astype(jnp.int32)


def draw_neighbours_first(key, part):
    return neighbour_draw(jax.random.fold_in(key, 11))


def draw_neighbours_second(key, part):
    return neighbour_draw(jax.random.fold_in(key, 12))


def draw_sends_first(key, part):
    return send_draw(jax.random.fold_in(key, 21))


def draw_sends_second(key, part):
    return send_draw(jax.random.fold_in(key, 22))


def segment_slots(key):
    key_one, key_two, key_three, key_four = jax.random.split(key, 4)
    members = jnp.arange(N_GROUP, dtype=jnp.int32)
    raw = jnp.maximum(jax.random.randint(key_one, (N_GROUP, N_GROUP), 0, 5) - 2, 0)
    upper = jnp.triu(raw, 1)
    amounts = upper + upper.T
    first = jax.random.randint(key_two, (), 0, N_GROUP)
    second = (first + 1 + jax.random.randint(key_three, (), 0, N_GROUP - 1)) % N_GROUP
    forced = (members[:, None] == first) & (members[None, :] == second) | (members[:, None] == second) & (members[None, :] == first)
    amounts = jnp.where(forced, MOVE_CAP, amounts)
    offsets = jnp.cumsum(amounts, axis=1) - amounts
    perms = jax.vmap(lambda inner: jax.random.permutation(inner, BLK_DEV))(jax.random.split(key_four, N_GROUP)).astype(jnp.int32)
    ranks = jnp.arange(BLK_DEV, dtype=jnp.int32)
    inside = (ranks[None, None, :] >= offsets[:, :, None]) & (ranks[None, None, :] < (offsets + amounts)[:, :, None])
    partner = jnp.sum(inside.astype(jnp.int32) * members[None, :, None], axis=1)
    moving = jnp.sum(inside.astype(jnp.int32), axis=1) > 0
    within = ranks[None, :] - jnp.take_along_axis(offsets, partner, axis=1)
    partner_rank = jnp.clip(offsets[partner, members[:, None]] + within, 0, BLK_DEV - 1)
    partner_slot = perms[partner, partner_rank]
    at_rank = jnp.where(moving, partner * BLK_DEV + partner_slot, members[:, None] * BLK_DEV + perms)
    inverse = jnp.argsort(perms, axis=1)
    return jnp.take_along_axis(at_rank, inverse, axis=1)


def draw_new_slot(key, part):
    keys = jax.random.split(jax.random.fold_in(key, 31), N_CURVE)
    table = jax.vmap(segment_slots)(keys)
    return jnp.transpose(table, (1, 0, 2)).reshape(N_GROUP, NBLK).astype(jnp.int32)


def place_ends(array, own_key, least, largest):
    place = [jax.random.randint(jax.random.fold_in(own_key, axis), (), 0, length) for axis, length in enumerate(array.shape)]
    widest = array.shape.index(max(array.shape))
    neighbour = place[:widest] + [(place[widest] + 1) % array.shape[widest]] + place[widest + 1:]
    return array.at[tuple(place)].set(least).at[tuple(neighbour)].set(largest)


def block_scale(own_key, extent, shards, smallest, largest):
    factor_of = 1.0
    for dim, shards_of in shards:
        steps = jax.random.uniform(jax.random.fold_in(jax.random.fold_in(own_key, 6), dim), (shards_of,), jnp.float32, smallest / len(shards), largest / len(shards))
        factor_of = factor_of * jnp.repeat(jnp.exp(steps), extent[dim] // shards_of).reshape((-1,) + (1,) * (len(extent) - 1 - dim))
    return factor_of


def bell_draw(stream_key, extent, deviation, most, pieces=(), kind=jnp.bfloat16):
    drawn = jax.random.normal(stream_key, extent, jnp.float32) * deviation
    if len(pieces) > 0:
        drawn = block_scale(stream_key, extent, pieces, -0.22, 0.18) * drawn
    return jnp.clip(drawn, min=-most, max=most).astype(kind)


def setup_inputs(seed: int = 0) -> dict:
    streams_of = jax.random.split(jax.random.key(seed), 10)
    return {
        "positions": draw_positions(jax.random.fold_in(streams_of[9], 71), 0),
        "velocities": bell_draw(streams_of[1], (N_GROUP, NBLK, 3, P_SIZE), 0.5, 3.0, ((0, 8), (1, 128)), jnp.float32),
        "masses": jnp.clip(jnp.exp(math.log(0.03) - 2.3025851 * jax.random.uniform(streams_of[2], (N_GROUP, NBLK, P_SIZE), jnp.float32) ** block_scale(streams_of[2], (N_GROUP, NBLK, P_SIZE), ((0, 8), (1, 128)), -0.2, 0.2)), 0.003, 0.03),
        "counts": place_ends(jax.random.randint(streams_of[3], (N_GROUP, NBLK), P_SIZE // 2, P_SIZE + 1), jax.random.fold_in(streams_of[3], 1), P_SIZE // 2, P_SIZE).astype(jnp.int32),
        "neighbours_first": draw_neighbours_first(jax.random.fold_in(streams_of[9], 71), 0),
        "sends_first": draw_sends_first(jax.random.fold_in(streams_of[9], 71), 0),
        "new_slot": draw_new_slot(jax.random.fold_in(streams_of[9], 71), 0),
        "neighbours_second": draw_neighbours_second(jax.random.fold_in(streams_of[9], 71), 0),
        "sends_second": draw_sends_second(jax.random.fold_in(streams_of[9], 71), 0),
    }


KERNEL_SCALE = 4.0
SMOOTHING = 0.5
SOFTENING = 0.0025
BACKGROUND = 0.5
TIME_STEP = 0.1


def kernel_density(target_x, source_x, source_mass):
    offsets = [target_x[:, None, axis_id, :, None] - source_x[:, :, axis_id, None, :] for axis_id in range(3)]
    square = offsets[0] * offsets[0] + offsets[1] * offsets[1] + offsets[2] * offsets[2]
    weight = jnp.exp(-KERNEL_SCALE * square)
    return BACKGROUND + jnp.sum(weight * source_mass[:, :, None, :], axis=(1, 3))


def kernel_force(target_x, target_v, target_rho, source_x, source_v, source_mass, source_rho):
    offsets = [target_x[:, None, axis_id, :, None] - source_x[:, :, axis_id, None, :] for axis_id in range(3)]
    square = offsets[0] * offsets[0] + offsets[1] * offsets[1] + offsets[2] * offsets[2]
    approach = offsets[0] * (target_v[:, None, 0, :, None] - source_v[:, :, 0, None, :])
    approach = approach + offsets[1] * (target_v[:, None, 1, :, None] - source_v[:, :, 1, None, :])
    approach = approach + offsets[2] * (target_v[:, None, 2, :, None] - source_v[:, :, 2, None, :])
    weight = jnp.exp(-KERNEL_SCALE * square)
    closing = SMOOTHING * jnp.minimum(approach, 0.0) / (square + SOFTENING)
    mine = target_rho[:, None, :, None]
    theirs = source_rho[:, :, None, :]
    factor = source_mass[:, :, None, :] * (1.0 / mine + 1.0 / theirs - closing / (0.5 * (mine + theirs)))
    factor = factor * (2.0 * KERNEL_SCALE) * weight
    return jnp.stack([jnp.sum(factor * offsets[axis_id], axis=(1, 3)) for axis_id in range(3)], axis=1)


def batched(function, arrays):
    shaped = tuple(item.reshape((item.shape[0] // 4, 4) + item.shape[1:]) for item in arrays)
    result = lax.map(lambda piece: function(*piece), shaped)
    return result.reshape((-1,) + result.shape[2:])


def candidate_table(field, sends):
    outgoing = jax.vmap(lambda blocks, picks: jnp.take(blocks, picks, axis=0))(field, sends)
    half = sends.shape[1] // 2
    lower = jnp.roll(outgoing, 1, axis=0)[:, half:]
    upper = jnp.roll(outgoing, -1, axis=0)[:, :half]
    return jnp.concatenate([field, lower, upper], axis=1)


def group_step(positions, velocities, mass_live, neighbours, sends):
    segments = positions.shape[0] // BLK_DEV
    shape_of = lambda item: item.reshape((segments, BLK_DEV) + item.shape[1:])
    picks = sends.reshape(segments, -1)
    own = jnp.broadcast_to(jnp.arange(BLK_DEV, dtype=jnp.int32)[None, :, None], (segments, BLK_DEV, 1))
    index = jnp.concatenate([own, shape_of(neighbours).astype(jnp.int32)], axis=2)

    def pick(field):
        table = candidate_table(shape_of(field), picks)
        chosen = jax.vmap(lambda block_table, rows: jnp.take(block_table, rows, axis=0))(table, index)
        return chosen.reshape((segments * BLK_DEV,) + chosen.shape[2:])

    source_x = pick(positions)
    source_m = pick(mass_live)
    density = batched(kernel_density, (positions, source_x, source_m))
    accel = batched(kernel_force, (positions, velocities, density, source_x, pick(velocities), source_m, pick(density)))
    new_velocity = velocities + TIME_STEP * accel
    new_position = positions + TIME_STEP * new_velocity
    return new_position, new_velocity, density


def migrate(field, new_slot):
    groups, blocks = field.shape[0], field.shape[1]
    segments = blocks // BLK_DEV
    rest = field.shape[2:]
    moved = field.reshape((groups, segments, BLK_DEV) + rest)
    moved = jnp.moveaxis(moved, 0, 1).reshape((segments, groups * BLK_DEV) + rest)
    target = jnp.moveaxis(new_slot.reshape(groups, segments, BLK_DEV), 0, 1).reshape(segments, groups * BLK_DEV)
    rows = jnp.arange(segments, dtype=jnp.int32)[:, None]
    placed = jnp.zeros_like(moved).at[rows, target.astype(jnp.int32)].set(moved)
    placed = placed.reshape((segments, groups, BLK_DEV) + rest)
    return jnp.moveaxis(placed, 1, 0).reshape(field.shape)


def reference(positions, velocities, masses, counts, neighbours_first, sends_first, new_slot, neighbours_second, sends_second):
    slots = jnp.arange(masses.shape[-1], dtype=jnp.int32)
    live = (slots[None, None, :] < counts[:, :, None]).astype(masses.dtype)
    mass_live = masses * live
    first_x, first_v, first_rho = lax.map(lambda item: group_step(*item), (positions, velocities, mass_live, neighbours_first, sends_first))
    moved_x = migrate(first_x, new_slot)
    moved_v = migrate(first_v, new_slot)
    moved_m = migrate(mass_live, new_slot)
    final_x, final_v, final_rho = lax.map(lambda item: group_step(*item), (moved_x, moved_v, moved_m, neighbours_second, sends_second))
    return final_x, final_v, final_rho
```

```python
import math

import jax
import jax.numpy as jnp
from jax import lax
from jax.experimental import pallas as pl
from jax.experimental.pallas import tpu as pltpu
from jax.sharding import PartitionSpec as P

SOFTENING = 0.0025
BACKGROUND = 0.5
TIME_STEP = 0.1
SPACING = 0.6

BLOCKS = 16
HALO = 4
NBR = 6
CANDIDATES = BLOCKS + 2 * HALO
LANES = 128
FEATURES = 64
MOVES = 2
KAPPA = 4.0 * math.log2(math.e)
MASS_SCALE = 2.0 ** (KAPPA * SOFTENING)
FORCE_SCALE = 8.0 * MASS_SCALE

F32 = jnp.float32
BF16 = jnp.bfloat16
VMEM = pl.BlockSpec(memory_space=pltpu.VMEM)
SMEM = pl.BlockSpec(memory_space=pltpu.SMEM)


def rounded(value):
    return value.astype(BF16).astype(F32)


def split(value):
    high = rounded(value)
    rest = value - high
    middle = rounded(rest)
    return high, middle, rest - middle


def tile_rows():
    return lax.broadcasted_iota(jnp.int32, (8, LANES), 0)


def three_rows(rows, first, parts):
    return jnp.where(
        rows == first, parts[0], jnp.where(rows == first + 1, parts[1], jnp.where(rows == first + 2, parts[2], 0.0))
    )


def local_tile(tile, base, rows):
    shifted = jnp.where(rows == 0, tile - base, tile)
    return jnp.where(rows < 6, shifted, 0.0)


def swapped(local, rows):
    down = pltpu.roll(local, 5, axis=0)
    up = pltpu.roll(local, 3, axis=0)
    return jnp.where(rows < 3, down, jnp.where(rows < 6, up, 0.0))


def quadratics(local, other, rows):
    square = jnp.sum(jnp.where(rows < 3, local * local, 0.0), axis=0, keepdims=True)
    mixed = jnp.sum(jnp.where(rows < 3, local * other, 0.0), axis=0, keepdims=True)
    return square, mixed


def source_features(tile, base, rows):
    local = local_tile(tile, base, rows)
    other = swapped(local, rows)
    square, mixed = quadratics(local, other, rows)
    near = split(jnp.where(rows < 3, (2.0 * KAPPA) * local, 0.0))
    flow = split(-KAPPA * other)
    minus = jnp.where(rows < 3, -1.0, 0.0)
    plus = jnp.where((rows >= 3) & (rows < 6), 1.0, 0.0)
    last_near = three_rows(rows, 0, split(-KAPPA * (square + SOFTENING)))
    last_flow = three_rows(rows, 0, split(KAPPA * mixed))
    first = jnp.concatenate([near[0], near[1], near[2], near[0], near[1], near[0], minus, last_near], axis=0)
    second = jnp.concatenate([flow[0], flow[1], flow[2], flow[0], flow[1], flow[0], plus, last_flow], axis=0)
    mass = tile[6:7] * FORCE_SCALE
    weights = split(mass * jnp.where(rows < 3, local, jnp.where(rows == 3, 1.0, 0.0)))
    summed = jnp.concatenate([weights[0], weights[1], weights[2], jnp.zeros_like(local)], axis=0)
    return first.astype(BF16), second.astype(BF16), summed.astype(BF16)


def target_features(tile, base, rows):
    local = local_tile(tile, base, rows)
    other = swapped(local, rows)
    square, mixed = quadratics(local, other, rows)
    high, middle, low = split(local)
    quadratic = three_rows(rows, 0, split(KAPPA * square)) + three_rows(rows, 3, split(KAPPA * mixed))
    ones = jnp.where(rows < 3, 1.0, 0.0)
    stacked = jnp.concatenate([high, high, high, middle, middle, low, quadratic, ones], axis=0)
    return stacked.T.astype(BF16)


def base_of_segment():
    return SPACING * lax.axis_index("curve").astype(F32)


def list_blocks(table_ref, picks_ref, low_ref, high_ref):
    for h in range(HALO):
        low_ref[h] = table_ref[picks_ref[0, h]]
        high_ref[h] = table_ref[picks_ref[0, HALO + h]]


def gather_kernel(x_ref, v_ref, m_ref, counts_ref, picks_ref, table_ref, low_ref, high_ref, flat_ref):
    for axis_id in range(3):
        flat_ref[pl.ds(axis_id, BLOCKS, stride=8), :] = x_ref[axis_id]
        flat_ref[pl.ds(3 + axis_id, BLOCKS, stride=8), :] = v_ref[axis_id]
    lane = lax.broadcasted_iota(jnp.int32, (1, LANES), 1)
    for b in range(BLOCKS):
        live = jnp.where(lane < counts_ref[0, b], m_ref[pl.ds(b, 1), :], 0.0)
        flat_ref[pl.ds(8 * b + 6, 1), :] = live
        flat_ref[pl.ds(8 * b + 7, 1), :] = jnp.zeros_like(live)
    for b in range(BLOCKS):
        table_ref[b] = flat_ref[pl.ds(8 * b, 8), :]
    list_blocks(table_ref, picks_ref, low_ref, high_ref)


def density_kernel(
    table_ref, below_ref, above_ref, near_ref, picks_ref,
    rho_ref, low_ref, high_ref, pair_ref, target_ref, sum_ref, mass_ref,
):
    base = base_of_segment()
    rows = tile_rows()

    def put(tile, at):
        first, second, summed = source_features(tile, base, rows)
        pair_ref[at, :, 0:LANES] = first
        pair_ref[at, :, LANES : 2 * LANES] = second
        sum_ref[at] = summed
        mass_ref[at] = tile[6:7] * MASS_SCALE

    def own(b, carry):
        tile = table_ref[b]
        put(tile, b)
        target_ref[b] = target_features(tile, base, rows)
        return carry

    lax.fori_loop(0, BLOCKS, own, 0, unroll=4)
    for h in range(HALO):
        put(below_ref[h], BLOCKS + h)
        put(above_ref[h], BLOCKS + HALO + h)

    ones = jnp.ones((8, LANES), F32)

    def target(j, carry):
        left = target_ref[j]
        sources = [j] + [near_ref[n, 0, j] for n in range(NBR)]
        total = jnp.zeros((LANES, LANES), F32)
        for start in range(0, NBR + 1, 2):
            chosen = sources[start : start + 2]
            right = [pair_ref[s, :, 0:LANES] for s in chosen]
            right = right[0] if len(right) == 1 else jnp.concatenate(right, axis=1)
            weight = jnp.exp2(jnp.dot(left, right, preferred_element_type=F32))
            for n, s in enumerate(chosen):
                total = total + weight[:, n * LANES : (n + 1) * LANES] * mass_ref[s]
        row = lax.dot_general(
            ones, total, (((1,), (1,)), ((), ())), precision=lax.Precision.HIGHEST, preferred_element_type=F32
        )
        rho_ref[j] = BACKGROUND + row[0:1]
        return carry

    lax.fori_loop(0, BLOCKS, target, 0)
    for h in range(HALO):
        low_ref[pl.ds(h, 1), :] = rho_ref[picks_ref[0, h]]
        high_ref[pl.ds(h, 1), :] = rho_ref[picks_ref[0, HALO + h]]


def advance(table_ref, rho_ref, below_ref, above_ref, near_ref, pair_ref, target_ref, sum_ref, all_rho, columns, done):
    base = base_of_segment()
    rows = tile_rows()
    flat = jnp.concatenate([rho_ref[b] for b in range(BLOCKS)], axis=0)
    for b in range(BLOCKS):
        all_rho[b] = rho_ref[b]
    for h in range(HALO):
        all_rho[BLOCKS + h] = below_ref[pl.ds(h, 1), :]
        all_rho[BLOCKS + HALO + h] = above_ref[pl.ds(h, 1), :]
    columns[...] = jnp.concatenate([flat, jnp.ones((LANES - BLOCKS, LANES), F32)], axis=0).T
    lane = lax.broadcasted_iota(jnp.int32, (LANES, LANES), 1)

    def target(j, carry):
        left = target_ref[j]
        mine = jnp.sum(jnp.where(lane == j, columns[...], 0.0), axis=1, keepdims=True)
        mine_inverse = 1.0 / mine
        sources = [j] + [near_ref[n, 0, j] for n in range(NBR)]
        total = jnp.zeros((32, LANES), F32)
        for s in sources:
            product = jnp.dot(left, pair_ref[s], preferred_element_type=F32)
            distance = product[:, 0:LANES]
            approach = product[:, LANES : 2 * LANES]
            theirs = all_rho[s]
            closing = jnp.minimum(approach, 0.0) / (distance * (mine + theirs))
            factor = jnp.exp2(distance) * (closing + (mine_inverse + 1.0 / theirs))
            high = factor.astype(BF16)
            low = (factor - high.astype(F32)).astype(BF16)
            weights = sum_ref[s]
            for part in (high, low):
                total = total + lax.dot_general(
                    weights, part, (((1,), (1,)), ((), ())), preferred_element_type=F32
                )
        sums = total[0:8] + total[8:16] + total[16:24]
        tile = table_ref[j]
        local = local_tile(tile, base, rows)
        accel = jnp.where(rows < 3, local * sums[3:4] - sums, 0.0)
        kicked = tile + TIME_STEP * pltpu.roll(accel, 3, axis=0)
        drift = pltpu.roll(kicked, 5, axis=0)
        done(j, jnp.where(rows < 3, kicked + TIME_STEP * drift, kicked))
        return carry

    lax.fori_loop(0, BLOCKS, target, 0)


def force_move_kernel(
    table_ref, rho_ref, below_ref, above_ref, near_ref, pair_ref, target_ref, sum_ref, slot_ref,
    stay_ref, send_ref, all_rho, columns, filled,
):
    me = lax.axis_index("group")
    rows = tile_rows()
    groups = send_ref.shape[0]
    for g in range(groups):
        filled[g] = 0
        for k in range(MOVES):
            send_ref[g, k] = jnp.full((8, LANES), -1.0, F32)
    for b in range(BLOCKS):
        stay_ref[b] = jnp.zeros((8, LANES), F32)

    def done(b, tile):
        owner = slot_ref[0, b] // BLOCKS
        slot = slot_ref[0, b] % BLOCKS
        tagged = jnp.where(rows == 7, jnp.full((8, LANES), slot, jnp.int32).astype(F32), tile)

        @pl.when(owner == me)
        def _():
            stay_ref[slot] = tagged

        @pl.when(owner != me)
        def _():
            place = jnp.minimum(filled[owner], MOVES - 1)
            send_ref[owner, place] = tagged
            filled[owner] = place + 1

    advance(
        table_ref, rho_ref, below_ref, above_ref, near_ref, pair_ref, target_ref, sum_ref, all_rho, columns, done
    )


def arrive_kernel(stay_ref, arrived_ref, picks_ref, table_ref, low_ref, high_ref):
    groups = arrived_ref.shape[0]
    tiles = [arrived_ref[g, k] for g in range(groups) for k in range(MOVES)]
    tags = [jnp.broadcast_to(tile[7:8], (8, LANES)) for tile in tiles]
    for s in range(BLOCKS):
        value = stay_ref[s]
        for tile, tag in zip(tiles, tags):
            value = jnp.where(tag == float(s), tile, value)
        table_ref[s] = value
    list_blocks(table_ref, picks_ref, low_ref, high_ref)


def force_out_kernel(
    table_ref, rho_ref, below_ref, above_ref, near_ref, pair_ref, target_ref, sum_ref,
    x_ref, v_ref, all_rho, columns, flat_ref,
):
    def done(b, tile):
        flat_ref[pl.ds(pl.multiple_of(8 * b, 8), 8), :] = tile

    advance(
        table_ref, rho_ref, below_ref, above_ref, near_ref, pair_ref, target_ref, sum_ref, all_rho, columns, done
    )
    for axis_id in range(3):
        x_ref[axis_id] = flat_ref[pl.ds(axis_id, BLOCKS, stride=8), :]
        v_ref[axis_id] = flat_ref[pl.ds(3 + axis_id, BLOCKS, stride=8), :]


def shape(*dims, dtype=F32):
    return jax.ShapeDtypeStruct(dims, dtype)


TABLE = shape(BLOCKS, 8, LANES)
LISTED = shape(HALO, 8, LANES)


def call(kernel, name, out_shape, in_specs, scratch=(), flops=0):
    return pl.pallas_call(
        kernel,
        name=name,
        out_shape=out_shape,
        in_specs=in_specs,
        out_specs=[VMEM] * len(out_shape),
        scratch_shapes=list(scratch),
        cost_estimate=pl.CostEstimate(flops=flops, bytes_accessed=200000, transcendentals=0),
    )


def exchange(low, high):
    count = lax.axis_size("curve")
    forward = [(i, (i + 1) % count) for i in range(count)]
    backward = [(target, source) for source, target in forward]
    return lax.ppermute(high, "curve", forward), lax.ppermute(low, "curve", backward)


def half_step(table, below, above, near, picks):
    rho, low, high, pairs, targets, sums = call(
        density_kernel,
        "density",
        (
            shape(BLOCKS, 1, LANES),
            shape(HALO, LANES),
            shape(HALO, LANES),
            shape(CANDIDATES, FEATURES, 2 * LANES, dtype=BF16),
            shape(BLOCKS, LANES, FEATURES, dtype=BF16),
            shape(CANDIDATES, 32, LANES, dtype=BF16),
        ),
        [VMEM, VMEM, VMEM, SMEM, SMEM],
        [pltpu.VMEM((CANDIDATES, 1, LANES), F32)],
    )(table, below, above, near, picks)
    rho_below, rho_above = exchange(low, high)
    return (table, rho, rho_below, rho_above, near, pairs, targets, sums)


FORCE_SPECS = [VMEM, VMEM, VMEM, VMEM, SMEM, VMEM, VMEM, VMEM]
FORCE_SCRATCH = [pltpu.VMEM((CANDIDATES, 1, LANES), F32), pltpu.VMEM((LANES, LANES), F32)]


def body(x, v, masses, counts, near_first, picks_first, new_slot, near_second, picks_second):
    groups = lax.axis_size("group")
    near_first = jnp.transpose(near_first, (2, 0, 1))
    near_second = jnp.transpose(near_second, (2, 0, 1))
    table, low, high = call(
        gather_kernel,
        "gather",
        (TABLE, LISTED, LISTED),
        [VMEM, VMEM, VMEM, SMEM, SMEM],
        [pltpu.VMEM((8 * BLOCKS, LANES), F32)],
    )(jnp.transpose(x[0], (1, 0, 2)), jnp.transpose(v[0], (1, 0, 2)), masses[0], counts, picks_first)
    below, above = exchange(low, high)
    stay, send = call(
        force_move_kernel,
        "force_move",
        (TABLE, shape(groups, MOVES, 8, LANES)),
        FORCE_SPECS + [SMEM],
        FORCE_SCRATCH + [pltpu.SMEM((groups,), jnp.int32)],
    )(*half_step(table, below, above, near_first, picks_first), new_slot)
    arrived = lax.all_to_all(send, "group", 0, 0)
    table, low, high = call(
        arrive_kernel, "arrive", (TABLE, LISTED, LISTED), [VMEM, VMEM, SMEM]
    )(stay, arrived, picks_second)
    below, above = exchange(low, high)
    state = half_step(table, below, above, near_second, picks_second)
    x_out, v_out = call(
        force_out_kernel,
        "force_out",
        (shape(3, BLOCKS, LANES), shape(3, BLOCKS, LANES)),
        FORCE_SPECS,
        FORCE_SCRATCH + [pltpu.VMEM((8 * BLOCKS, LANES), F32)],
    )(*state)
    rho = state[1].reshape(1, BLOCKS, LANES)
    return jnp.transpose(x_out, (1, 0, 2))[None], jnp.transpose(v_out, (1, 0, 2))[None], rho


def solution(mesh):
    in_specs = (
        P("group", "curve", None, None),
        P("group", "curve", None, None),
        P("group", "curve", None),
        P("group", "curve"),
        P("group", "curve", None),
        P("group", "curve"),
        P("group", "curve"),
        P("group", "curve", None),
        P("group", "curve"),
    )
    out_specs = (
        P("group", "curve", None, None),
        P("group", "curve", None, None),
        P("group", "curve", None),
    )
    return jax.shard_map(body, mesh=mesh, in_specs=in_specs, out_specs=out_specs, check_vma=False)
```

```python
import math

import jax
import jax.numpy as jnp
from jax import lax
from jax.experimental import pallas as pl
from jax.experimental.pallas import tpu as pltpu
from jax.sharding import PartitionSpec as P

SOFTENING = 0.0025
BACKGROUND = 0.5
TIME_STEP = 0.1
SPACING = 0.6

BLOCKS = 16
HALO = 4
NBR = 6
CANDIDATES = BLOCKS + 2 * HALO
LANES = 128
FEATURES = 64
MOVES = 2
KAPPA = 4.0 * math.log2(math.e)
MASS_SCALE = 2.0 ** (KAPPA * SOFTENING)
FORCE_SCALE = 8.0 * MASS_SCALE
NO_MASS = -4096.0

F32 = jnp.float32
BF16 = jnp.bfloat16
VMEM = pl.BlockSpec(memory_space=pltpu.VMEM)
SMEM = pl.BlockSpec(memory_space=pltpu.SMEM)


def rounded(value):
    return value.astype(BF16).astype(F32)


def split(value):
    high = rounded(value)
    rest = value - high
    middle = rounded(rest)
    return high, middle, rest - middle


def tile_rows():
    return lax.broadcasted_iota(jnp.int32, (8, LANES), 0)


def three_rows(rows, first, parts):
    return jnp.where(
        rows == first, parts[0], jnp.where(rows == first + 1, parts[1], jnp.where(rows == first + 2, parts[2], 0.0))
    )


def local_tile(tile, base, rows):
    shifted = jnp.where(rows == 0, tile - base, tile)
    return jnp.where(rows < 6, shifted, 0.0)


def swapped(local, rows):
    down = pltpu.roll(local, 5, axis=0)
    up = pltpu.roll(local, 3, axis=0)
    return jnp.where(rows < 3, down, jnp.where(rows < 6, up, 0.0))


def quadratics(local, other, rows):
    square = jnp.sum(jnp.where(rows < 3, local * local, 0.0), axis=0, keepdims=True)
    mixed = jnp.sum(jnp.where(rows < 3, local * other, 0.0), axis=0, keepdims=True)
    return square, mixed


def target_features(tile, base, rows):
    local = local_tile(tile, base, rows)
    other = swapped(local, rows)
    square, mixed = quadratics(local, other, rows)
    near = split(jnp.where(rows < 3, (2.0 * KAPPA) * local, 0.0))
    flow = split(-KAPPA * other)
    minus = jnp.where(rows < 3, -1.0, 0.0)
    plus = jnp.where((rows >= 3) & (rows < 6), 1.0, 0.0)
    last_near = three_rows(rows, 0, split(-KAPPA * (square + SOFTENING)))
    last_flow = three_rows(rows, 0, split(KAPPA * mixed))
    near = [near[0], near[1], near[2], near[0], near[1], near[0]]
    flow = [flow[0], flow[1], flow[2], flow[0], flow[1], flow[0]]
    distance = jnp.concatenate(near + [minus, last_near], axis=0)
    approach = jnp.concatenate(flow + [plus, last_flow], axis=0)
    weighted = jnp.concatenate(
        near + [jnp.where(rows >= 6, 1.0, minus), jnp.where(rows == 3, 1.0, last_near)], axis=0
    )
    return distance.astype(BF16), approach.astype(BF16), weighted.astype(BF16)


def source_features(tile, base, rows):
    local = local_tile(tile, base, rows)
    other = swapped(local, rows)
    square, mixed = quadratics(local, other, rows)
    high, middle, low = split(local)
    mass = tile[6:7]
    alive = mass > 0.0
    exponent = jnp.where(alive, jnp.log2(jnp.where(alive, mass, 1.0)) + KAPPA * SOFTENING, NO_MASS)
    exponents = split(exponent)
    quadratic = three_rows(rows, 0, split(KAPPA * square)) + three_rows(rows, 3, split(KAPPA * mixed))
    quadratic = jnp.where(rows == 6, exponents[0], jnp.where(rows == 7, exponents[1], quadratic))
    ones = jnp.where(rows < 3, 1.0, jnp.where(rows == 3, exponents[2], 0.0))
    stacked = jnp.concatenate([high, high, high, middle, middle, low, quadratic, ones], axis=0)
    weights = split((mass * FORCE_SCALE) * jnp.where(rows < 3, local, jnp.where(rows == 3, 1.0, 0.0)))
    summed = jnp.concatenate([weights[0], weights[1], weights[2], jnp.zeros_like(local)], axis=0).astype(BF16)
    return stacked.T.astype(BF16), jnp.concatenate([summed, summed], axis=1)


def base_of_segment():
    return SPACING * lax.axis_index("curve").astype(F32)


def list_blocks(table_ref, picks_ref, low_ref, high_ref):
    for h in range(HALO):
        low_ref[h] = table_ref[picks_ref[0, h]]
        high_ref[h] = table_ref[picks_ref[0, HALO + h]]


def gather_kernel(x_ref, v_ref, m_ref, counts_ref, picks_ref, table_ref, low_ref, high_ref, flat_ref):
    for axis_id in range(3):
        flat_ref[pl.ds(axis_id, BLOCKS, stride=8), :] = x_ref[axis_id]
        flat_ref[pl.ds(3 + axis_id, BLOCKS, stride=8), :] = v_ref[axis_id]
    lane = lax.broadcasted_iota(jnp.int32, (1, LANES), 1)
    for b in range(BLOCKS):
        live = jnp.where(lane < counts_ref[0, b], m_ref[pl.ds(b, 1), :], 0.0)
        flat_ref[pl.ds(8 * b + 6, 1), :] = live
        flat_ref[pl.ds(8 * b + 7, 1), :] = jnp.zeros_like(live)
    for b in range(BLOCKS):
        table_ref[b] = flat_ref[pl.ds(8 * b, 8), :]
    list_blocks(table_ref, picks_ref, low_ref, high_ref)


def density_kernel(
    table_ref, below_ref, above_ref, near_ref, picks_ref,
    rho_ref, low_ref, high_ref, target_ref, source_ref, sum_ref,
):
    base = base_of_segment()
    rows = tile_rows()

    def put(tile, at):
        features, summed = source_features(tile, base, rows)
        source_ref[at] = features
        sum_ref[at] = summed

    def own(b, carry):
        tile = table_ref[b]
        put(tile, b)
        parts = target_features(tile, base, rows)
        for n in range(3):
            target_ref[b, :, n * LANES : (n + 1) * LANES] = parts[n]
        return carry

    lax.fori_loop(0, BLOCKS, own, 0, unroll=4)
    for h in range(HALO):
        put(below_ref[h], BLOCKS + h)
        put(above_ref[h], BLOCKS + HALO + h)

    def target(j, carry):
        right = target_ref[j, :, 2 * LANES : 3 * LANES]
        sources = [j] + [near_ref[n, 0, j] for n in range(NBR)]
        left = jnp.concatenate([source_ref[s] for s in sources], axis=0)
        weight = jnp.exp2(jnp.dot(left, right, preferred_element_type=F32))
        rho_ref[j] = BACKGROUND + jnp.sum(weight, axis=0, keepdims=True)
        return carry

    lax.fori_loop(0, BLOCKS, target, 0, unroll=2)
    for h in range(HALO):
        low_ref[pl.ds(h, 1), :] = rho_ref[picks_ref[0, h]]
        high_ref[pl.ds(h, 1), :] = rho_ref[picks_ref[0, HALO + h]]


def advance(
    table_ref, rho_ref, below_ref, above_ref, near_ref, target_ref, source_ref, sum_ref, rho_of, inverse_of, done
):
    base = base_of_segment()
    rows = tile_rows()
    flat = [rho_ref[b] for b in range(BLOCKS)] + [below_ref[...], above_ref[...], jnp.ones((8, LANES), F32)]
    flat = jnp.concatenate(flat, axis=0)
    across = flat.T
    for s in range(CANDIDATES):
        column = jnp.broadcast_to(across[:, s : s + 1], (LANES, LANES))
        rho_of[s] = column
        inverse_of[s] = 1.0 / column

    def target(j, carry):
        right = target_ref[j, :, 0 : 2 * LANES]
        mine = rho_ref[j]
        mine_inverse = 1.0 / mine
        sources = [j] + [near_ref[n, 0, j] for n in range(NBR)]
        wholes, lefts = [], []
        for s in sources:
            product = jnp.dot(source_ref[s], right, preferred_element_type=F32)
            distance = product[:, 0:LANES]
            approach = product[:, LANES : 2 * LANES]
            closing = jnp.minimum(approach, 0.0) / (distance * (mine + rho_of[s]))
            factor = jnp.exp2(distance) * (closing + (mine_inverse + inverse_of[s]))
            high = factor.astype(BF16)
            low = (factor - high.astype(F32)).astype(BF16)
            wholes += [high, low]
            lefts.append(sum_ref[s])
        total = jnp.dot(jnp.concatenate(lefts, axis=1), jnp.concatenate(wholes, axis=0), preferred_element_type=F32)
        sums = total[0:8] + total[8:16] + total[16:24]
        tile = table_ref[j]
        local = local_tile(tile, base, rows)
        accel = jnp.where(rows < 3, local * sums[3:4] - sums, 0.0)
        kicked = tile + TIME_STEP * pltpu.roll(accel, 3, axis=0)
        drift = pltpu.roll(kicked, 5, axis=0)
        done(j, jnp.where(rows < 3, kicked + TIME_STEP * drift, kicked))
        return carry

    lax.fori_loop(0, BLOCKS, target, 0, unroll=2)


def force_move_kernel(
    table_ref, rho_ref, below_ref, above_ref, near_ref, target_ref, source_ref, sum_ref, slot_ref,
    stay_ref, send_ref, rho_of, inverse_of, filled,
):
    me = lax.axis_index("group")
    rows = tile_rows()
    groups = send_ref.shape[0]
    for g in range(groups):
        filled[g] = 0
        for k in range(MOVES):
            send_ref[g, k] = jnp.full((8, LANES), -1.0, F32)
    for b in range(BLOCKS):
        stay_ref[b] = jnp.zeros((8, LANES), F32)

    def done(b, tile):
        owner = slot_ref[0, b] // BLOCKS
        slot = slot_ref[0, b] % BLOCKS
        tagged = jnp.where(rows == 7, jnp.full((8, LANES), slot, jnp.int32).astype(F32), tile)

        @pl.when(owner == me)
        def _():
            stay_ref[slot] = tagged

        @pl.when(owner != me)
        def _():
            place = jnp.minimum(filled[owner], MOVES - 1)
            send_ref[owner, place] = tagged
            filled[owner] = place + 1

    advance(
        table_ref, rho_ref, below_ref, above_ref, near_ref, target_ref, source_ref, sum_ref, rho_of, inverse_of, done
    )


def arrive_kernel(stay_ref, arrived_ref, picks_ref, table_ref, low_ref, high_ref):
    groups = arrived_ref.shape[0]
    tiles = [arrived_ref[g, k] for g in range(groups) for k in range(MOVES)]
    tags = [jnp.broadcast_to(tile[7:8], (8, LANES)) for tile in tiles]
    for s in range(BLOCKS):
        value = stay_ref[s]
        for tile, tag in zip(tiles, tags):
            value = jnp.where(tag == float(s), tile, value)
        table_ref[s] = value
    list_blocks(table_ref, picks_ref, low_ref, high_ref)


def force_out_kernel(
    table_ref, rho_ref, below_ref, above_ref, near_ref, target_ref, source_ref, sum_ref,
    x_ref, v_ref, rho_of, inverse_of, flat_ref,
):
    def done(b, tile):
        flat_ref[pl.ds(pl.multiple_of(8 * b, 8), 8), :] = tile

    advance(
        table_ref, rho_ref, below_ref, above_ref, near_ref, target_ref, source_ref, sum_ref, rho_of, inverse_of, done
    )
    for axis_id in range(3):
        x_ref[axis_id] = flat_ref[pl.ds(axis_id, BLOCKS, stride=8), :]
        v_ref[axis_id] = flat_ref[pl.ds(3 + axis_id, BLOCKS, stride=8), :]


def shape(*dims, dtype=F32):
    return jax.ShapeDtypeStruct(dims, dtype)


TABLE = shape(BLOCKS, 8, LANES)
LISTED = shape(HALO, 8, LANES)


def call(kernel, name, out_shape, in_specs, scratch=(), flops=0):
    return pl.pallas_call(
        kernel,
        name=name,
        out_shape=out_shape,
        in_specs=in_specs,
        out_specs=[VMEM] * len(out_shape),
        scratch_shapes=list(scratch),
        cost_estimate=pl.CostEstimate(flops=flops, bytes_accessed=200000, transcendentals=0),
        compiler_params=pltpu.CompilerParams(vmem_limit_bytes=16 << 20),
    )


def exchange(low, high):
    count = lax.axis_size("curve")
    forward = [(i, (i + 1) % count) for i in range(count)]
    backward = [(target, source) for source, target in forward]
    return lax.ppermute(high, "curve", forward), lax.ppermute(low, "curve", backward)


def half_step(table, below, above, near, picks):
    rho, low, high, targets, sources, sums = call(
        density_kernel,
        "density",
        (
            shape(BLOCKS, 1, LANES),
            shape(HALO, LANES),
            shape(HALO, LANES),
            shape(BLOCKS, FEATURES, 3 * LANES, dtype=BF16),
            shape(CANDIDATES, LANES, FEATURES, dtype=BF16),
            shape(CANDIDATES, 32, 2 * LANES, dtype=BF16),
        ),
        [VMEM, VMEM, VMEM, SMEM, SMEM],
    )(table, below, above, near, picks)
    rho_below, rho_above = exchange(low, high)
    return (table, rho, rho_below, rho_above, near, targets, sources, sums)


FORCE_SPECS = [VMEM, VMEM, VMEM, VMEM, SMEM, VMEM, VMEM, VMEM]
FORCE_SCRATCH = [pltpu.VMEM((CANDIDATES, LANES, LANES), F32)] * 2


def body(x, v, masses, counts, near_first, picks_first, new_slot, near_second, picks_second):
    groups = lax.axis_size("group")
    near_first = jnp.transpose(near_first, (2, 0, 1))
    near_second = jnp.transpose(near_second, (2, 0, 1))
    table, low, high = call(
        gather_kernel,
        "gather",
        (TABLE, LISTED, LISTED),
        [VMEM, VMEM, VMEM, SMEM, SMEM],
        [pltpu.VMEM((8 * BLOCKS, LANES), F32)],
    )(jnp.transpose(x[0], (1, 0, 2)), jnp.transpose(v[0], (1, 0, 2)), masses[0], counts, picks_first)
    below, above = exchange(low, high)
    stay, send = call(
        force_move_kernel,
        "force_move",
        (TABLE, shape(groups, MOVES, 8, LANES)),
        FORCE_SPECS + [SMEM],
        FORCE_SCRATCH + [pltpu.SMEM((groups,), jnp.int32)],
    )(*half_step(table, below, above, near_first, picks_first), new_slot)
    arrived = lax.all_to_all(send, "group", 0, 0)
    table, low, high = call(
        arrive_kernel, "arrive", (TABLE, LISTED, LISTED), [VMEM, VMEM, SMEM]
    )(stay, arrived, picks_second)
    below, above = exchange(low, high)
    state = half_step(table, below, above, near_second, picks_second)
    x_out, v_out = call(
        force_out_kernel,
        "force_out",
        (shape(3, BLOCKS, LANES), shape(3, BLOCKS, LANES)),
        FORCE_SPECS,
        FORCE_SCRATCH + [pltpu.VMEM((8 * BLOCKS, LANES), F32)],
    )(*state)
    rho = state[1].reshape(1, BLOCKS, LANES)
    return jnp.transpose(x_out, (1, 0, 2))[None], jnp.transpose(v_out, (1, 0, 2))[None], rho


def solution(mesh):
    in_specs = (
        P("group", "curve", None, None),
        P("group", "curve", None, None),
        P("group", "curve", None),
        P("group", "curve"),
        P("group", "curve", None),
        P("group", "curve"),
        P("group", "curve"),
        P("group", "curve", None),
        P("group", "curve"),
    )
    out_specs = (
        P("group", "curve", None, None),
        P("group", "curve", None, None),
        P("group", "curve", None),
    )
    return jax.shard_map(body, mesh=mesh, in_specs=in_specs, out_specs=out_specs, check_vma=False)
```

```python
import math

import jax
import jax.numpy as jnp
from jax import lax
from jax.experimental import pallas as pl
from jax.experimental.pallas import tpu as pltpu
from jax.sharding import PartitionSpec as P

SOFTENING = 0.0025
BACKGROUND = 0.5
TIME_STEP = 0.1
SPACING = 0.6

BLOCKS = 16
HALO = 4
NBR = 6
CANDIDATES = BLOCKS + 2 * HALO
LANES = 128
FEATURES = 64
MOVES = 2
GATHER_GRANT = 63_000_000
KAPPA = 4.0 * math.log2(math.e)
MASS_SCALE = 2.0 ** (KAPPA * SOFTENING)
FORCE_SCALE = 8.0 * MASS_SCALE
NO_MASS = -4096.0

F32 = jnp.float32
BF16 = jnp.bfloat16
VMEM = pl.BlockSpec(memory_space=pltpu.VMEM)
SMEM = pl.BlockSpec(memory_space=pltpu.SMEM)
HBM = pl.BlockSpec(memory_space=pltpu.HBM)


def rounded(value):
    return value.astype(BF16).astype(F32)


def split(value):
    high = rounded(value)
    rest = value - high
    middle = rounded(rest)
    return high, middle, rest - middle


def tile_rows():
    return lax.broadcasted_iota(jnp.int32, (8, LANES), 0)


def three_rows(rows, first, parts):
    return jnp.where(
        rows == first, parts[0], jnp.where(rows == first + 1, parts[1], jnp.where(rows == first + 2, parts[2], 0.0))
    )


def local_tile(tile, base, rows):
    shifted = jnp.where(rows == 0, tile - base, tile)
    return jnp.where(rows < 6, shifted, 0.0)


def swapped(local, rows):
    down = pltpu.roll(local, 5, axis=0)
    up = pltpu.roll(local, 3, axis=0)
    return jnp.where(rows < 3, down, jnp.where(rows < 6, up, 0.0))


def quadratics(local, other, rows):
    square = jnp.sum(jnp.where(rows < 3, local * local, 0.0), axis=0, keepdims=True)
    mixed = jnp.sum(jnp.where(rows < 3, local * other, 0.0), axis=0, keepdims=True)
    return square, mixed


def target_features(tile, base, rows):
    local = local_tile(tile, base, rows)
    other = swapped(local, rows)
    square, mixed = quadratics(local, other, rows)
    near = split(jnp.where(rows < 3, (2.0 * KAPPA) * local, 0.0))
    flow = split(-KAPPA * other)
    minus = jnp.where(rows < 3, -1.0, 0.0)
    plus = jnp.where((rows >= 3) & (rows < 6), 1.0, 0.0)
    last_near = three_rows(rows, 0, split(-KAPPA * (square + SOFTENING)))
    last_flow = three_rows(rows, 0, split(KAPPA * mixed))
    near = [near[0], near[1], near[2], near[0], near[1], near[0]]
    flow = [flow[0], flow[1], flow[2], flow[0], flow[1], flow[0]]
    distance = jnp.concatenate(near + [minus, last_near], axis=0)
    approach = jnp.concatenate(flow + [plus, last_flow], axis=0)
    weighted = jnp.concatenate(
        near + [jnp.where(rows >= 6, 1.0, minus), jnp.where(rows == 3, 1.0, last_near)], axis=0
    )
    return distance.astype(BF16), approach.astype(BF16), weighted.astype(BF16)


def source_features(tile, base, rows):
    local = local_tile(tile, base, rows)
    other = swapped(local, rows)
    square, mixed = quadratics(local, other, rows)
    high, middle, low = split(local)
    mass = tile[6:7]
    alive = mass > 0.0
    exponent = jnp.where(alive, jnp.log2(jnp.where(alive, mass, 1.0)) + KAPPA * SOFTENING, NO_MASS)
    exponents = split(exponent)
    quadratic = three_rows(rows, 0, split(KAPPA * square)) + three_rows(rows, 3, split(KAPPA * mixed))
    quadratic = jnp.where(rows == 6, exponents[0], jnp.where(rows == 7, exponents[1], quadratic))
    ones = jnp.where(rows < 3, 1.0, jnp.where(rows == 3, exponents[2], 0.0))
    stacked = jnp.concatenate([high, high, high, middle, middle, low, quadratic, ones], axis=0)
    weights = split((mass * FORCE_SCALE) * jnp.where(rows < 3, local, jnp.where(rows == 3, 1.0, 0.0)))
    summed = jnp.concatenate([weights[0], weights[1], weights[2], jnp.zeros_like(local)], axis=0).astype(BF16)
    return stacked.T.astype(BF16), jnp.concatenate([summed, summed], axis=1)


def base_of_segment():
    return SPACING * lax.axis_index("curve").astype(F32)


def parity():
    return lax.rem(lax.axis_index("curve"), 2)


def list_blocks(table_ref, picks_ref, outer_ref, inner_ref):
    odd = parity()
    for h in range(HALO):
        outer_ref[h] = table_ref[picks_ref[0, odd * HALO + h]]
        inner_ref[h] = table_ref[picks_ref[0, (1 - odd) * HALO + h]]


def gather_kernel(
    x_hbm, v_hbm, m_hbm, counts_hbm, picks_hbm,
    table_ref, outer_ref, inner_ref,
    x_ref, v_ref, m_ref, flat_ref, counts_ref, picks_ref, sems,
):
    pairs = ((x_hbm, x_ref), (v_hbm, v_ref), (m_hbm, m_ref), (counts_hbm, counts_ref), (picks_hbm, picks_ref))
    copies = [pltpu.make_async_copy(source, target, sems.at[n]) for n, (source, target) in enumerate(pairs)]
    for copy in copies:
        copy.start()
    for copy in copies:
        copy.wait()
    for axis_id in range(3):
        flat_ref[pl.ds(axis_id, BLOCKS, stride=8), :] = x_ref[axis_id]
        flat_ref[pl.ds(3 + axis_id, BLOCKS, stride=8), :] = v_ref[axis_id]
    lane = lax.broadcasted_iota(jnp.int32, (1, LANES), 1)
    for b in range(BLOCKS):
        live = jnp.where(lane < counts_ref[0, b], m_ref[pl.ds(b, 1), :], 0.0)
        flat_ref[pl.ds(8 * b + 6, 1), :] = live
        flat_ref[pl.ds(8 * b + 7, 1), :] = jnp.zeros_like(live)
    for b in range(BLOCKS):
        table_ref[b] = flat_ref[pl.ds(8 * b, 8), :]
    list_blocks(table_ref, picks_ref, outer_ref, inner_ref)


def density_kernel(table_ref, outer_ref, inner_ref, near_ref, picks_ref, *refs):
    rho_ref, outer_out_ref, inner_out_ref, target_ref, source_ref, sum_ref = refs[-6:]
    passed = (len(refs) - 6) // 2
    for n in range(passed):
        refs[passed + n][...] = refs[n][...]
    base = base_of_segment()
    odd = parity()
    rows = tile_rows()

    def put(tile, at):
        features, summed = source_features(tile, base, rows)
        source_ref[at] = features
        sum_ref[at] = summed

    def own(b, carry):
        tile = table_ref[b]
        put(tile, b)
        parts = target_features(tile, base, rows)
        for n in range(3):
            target_ref[b, :, n * LANES : (n + 1) * LANES] = parts[n]
        return carry

    lax.fori_loop(0, BLOCKS, own, 0, unroll=4)
    for h in range(HALO):
        put(outer_ref[h], BLOCKS + odd * HALO + h)
        put(inner_ref[h], BLOCKS + (1 - odd) * HALO + h)

    def target(j, carry):
        right = target_ref[j, :, 2 * LANES : 3 * LANES]
        sources = [j] + [near_ref[n, 0, j] for n in range(NBR)]
        left = jnp.concatenate([source_ref[s] for s in sources], axis=0)
        weight = jnp.exp2(jnp.dot(left, right, preferred_element_type=F32))
        rho_ref[j] = BACKGROUND + jnp.sum(weight, axis=0, keepdims=True)
        return carry

    lax.fori_loop(0, BLOCKS, target, 0, unroll=2)
    for h in range(HALO):
        outer_out_ref[pl.ds(h, 1), :] = rho_ref[picks_ref[0, odd * HALO + h]]
        inner_out_ref[pl.ds(h, 1), :] = rho_ref[picks_ref[0, (1 - odd) * HALO + h]]


def advance(
    table_ref, rho_ref, outer_ref, inner_ref, near_ref, target_ref, source_ref, sum_ref, rho_of, inverse_of, done
):
    base = base_of_segment()
    rows = tile_rows()
    even = parity() == 0
    outer, inner = outer_ref[...], inner_ref[...]
    below = jnp.where(even, outer, inner)
    above = jnp.where(even, inner, outer)
    flat = [rho_ref[b] for b in range(BLOCKS)] + [below, above, jnp.ones((8, LANES), F32)]
    flat = jnp.concatenate(flat, axis=0)
    across = flat.T
    for s in range(CANDIDATES):
        column = jnp.broadcast_to(across[:, s : s + 1], (LANES, LANES))
        rho_of[s] = column
        inverse_of[s] = 1.0 / column

    def target(j, carry):
        right = target_ref[j, :, 0 : 2 * LANES]
        mine = rho_ref[j]
        mine_inverse = 1.0 / mine
        sources = [j] + [near_ref[n, 0, j] for n in range(NBR)]
        wholes, lefts = [], []
        for s in sources:
            product = jnp.dot(source_ref[s], right, preferred_element_type=F32)
            distance = product[:, 0:LANES]
            approach = product[:, LANES : 2 * LANES]
            closing = jnp.minimum(approach, 0.0) / (distance * (mine + rho_of[s]))
            factor = jnp.exp2(distance) * (closing + (mine_inverse + inverse_of[s]))
            high = factor.astype(BF16)
            low = (factor - high.astype(F32)).astype(BF16)
            wholes += [high, low]
            lefts.append(sum_ref[s])
        total = jnp.dot(jnp.concatenate(lefts, axis=1), jnp.concatenate(wholes, axis=0), preferred_element_type=F32)
        sums = total[0:8] + total[8:16] + total[16:24]
        tile = table_ref[j]
        local = local_tile(tile, base, rows)
        accel = jnp.where(rows < 3, local * sums[3:4] - sums, 0.0)
        kicked = tile + TIME_STEP * pltpu.roll(accel, 3, axis=0)
        drift = pltpu.roll(kicked, 5, axis=0)
        done(j, jnp.where(rows < 3, kicked + TIME_STEP * drift, kicked))
        return carry

    lax.fori_loop(0, BLOCKS, target, 0, unroll=2)


def force_move_kernel(
    table_ref, rho_ref, outer_ref, inner_ref, near_ref, target_ref, source_ref, sum_ref, slot_hbm,
    stay_ref, send_ref, rho_of, inverse_of, filled, slot_ref, sem,
):
    copy = pltpu.make_async_copy(slot_hbm, slot_ref, sem)
    copy.start()
    me = lax.axis_index("group")
    rows = tile_rows()
    groups = send_ref.shape[0]
    for g in range(groups):
        filled[g] = 0
        for k in range(MOVES):
            send_ref[g, k] = jnp.full((8, LANES), -1.0, F32)
    for b in range(BLOCKS):
        stay_ref[b] = jnp.zeros((8, LANES), F32)
    copy.wait()

    def done(b, tile):
        owner = slot_ref[0, b] // BLOCKS
        slot = slot_ref[0, b] % BLOCKS
        tagged = jnp.where(rows == 7, jnp.full((8, LANES), slot, jnp.int32).astype(F32), tile)

        @pl.when(owner == me)
        def _():
            stay_ref[slot] = tagged

        @pl.when(owner != me)
        def _():
            place = jnp.minimum(filled[owner], MOVES - 1)
            send_ref[owner, place] = tagged
            filled[owner] = place + 1

    advance(
        table_ref, rho_ref, outer_ref, inner_ref, near_ref, target_ref, source_ref, sum_ref, rho_of, inverse_of, done
    )


def arrive_kernel(stay_ref, arrived_ref, picks_hbm, table_ref, outer_ref, inner_ref, picks_ref, sem):
    copy = pltpu.make_async_copy(picks_hbm, picks_ref, sem)
    copy.start()
    groups = arrived_ref.shape[0]
    tiles = [arrived_ref[g, k] for g in range(groups) for k in range(MOVES)]
    tags = [jnp.broadcast_to(tile[7:8], (8, LANES)) for tile in tiles]
    for s in range(BLOCKS):
        value = stay_ref[s]
        for tile, tag in zip(tiles, tags):
            value = jnp.where(tag == float(s), tile, value)
        table_ref[s] = value
    copy.wait()
    list_blocks(table_ref, picks_ref, outer_ref, inner_ref)


def force_out_kernel(
    table_ref, rho_ref, outer_ref, inner_ref, near_ref, target_ref, source_ref, sum_ref,
    x_ref, v_ref, rho_of, inverse_of, flat_ref,
):
    def done(b, tile):
        flat_ref[pl.ds(pl.multiple_of(8 * b, 8), 8), :] = tile

    advance(
        table_ref, rho_ref, outer_ref, inner_ref, near_ref, target_ref, source_ref, sum_ref, rho_of, inverse_of, done
    )
    for axis_id in range(3):
        x_ref[axis_id] = flat_ref[pl.ds(axis_id, BLOCKS, stride=8), :]
        v_ref[axis_id] = flat_ref[pl.ds(3 + axis_id, BLOCKS, stride=8), :]


def shape(*dims, dtype=F32):
    return jax.ShapeDtypeStruct(dims, dtype)


TABLE = shape(BLOCKS, 8, LANES)
LISTED = shape(HALO, 8, LANES)


def call(kernel, name, out_shape, in_specs, scratch=(), flops=0, grant=16 << 20):
    return pl.pallas_call(
        kernel,
        name=name,
        out_shape=out_shape,
        in_specs=in_specs,
        out_specs=[VMEM] * len(out_shape),
        scratch_shapes=list(scratch),
        cost_estimate=pl.CostEstimate(flops=flops, bytes_accessed=200000, transcendentals=0),
        compiler_params=pltpu.CompilerParams(vmem_limit_bytes=grant),
    )


def exchange(outer, inner):
    count = lax.axis_size("curve")
    odd_first = [(i, (i + 1) % count) for i in range(1, count, 2)]
    even_first = [(i, i + 1) for i in range(0, count, 2)]
    both = lambda pairs: pairs + [(target, source) for source, target in pairs]
    return lax.ppermute(outer, "curve", both(odd_first)), lax.ppermute(inner, "curve", both(even_first))


def half_step(table, outer, inner, near, picks, passed=()):
    *passed, rho, outer_rho, inner_rho, targets, sources, sums = call(
        density_kernel,
        "density",
        tuple(shape(*item.shape, dtype=item.dtype) for item in passed)
        + (
            shape(BLOCKS, 1, LANES),
            shape(HALO, LANES),
            shape(HALO, LANES),
            shape(BLOCKS, FEATURES, 3 * LANES, dtype=BF16),
            shape(CANDIDATES, LANES, FEATURES, dtype=BF16),
            shape(CANDIDATES, 32, 2 * LANES, dtype=BF16),
        ),
        [VMEM, VMEM, VMEM, SMEM, SMEM] + [VMEM] * len(passed),
    )(table, outer, inner, near, picks, *passed)
    outer_rho, inner_rho = exchange(outer_rho, inner_rho)
    return (table, rho, outer_rho, inner_rho, near, targets, sources, sums), passed


FORCE_SPECS = [VMEM, VMEM, VMEM, VMEM, SMEM, VMEM, VMEM, VMEM]
FORCE_SCRATCH = [pltpu.VMEM((CANDIDATES, LANES, LANES), F32)] * 2


def body(x, v, masses, counts, near_first, picks_first, new_slot, near_second, picks_second):
    groups = lax.axis_size("group")
    near_first = jnp.transpose(near_first, (2, 0, 1))
    near_second = jnp.transpose(near_second, (2, 0, 1))
    table, outer, inner = call(
        gather_kernel,
        "gather",
        (TABLE, LISTED, LISTED),
        [HBM] * 5,
        [
            pltpu.VMEM((3, BLOCKS, LANES), F32),
            pltpu.VMEM((3, BLOCKS, LANES), F32),
            pltpu.VMEM((BLOCKS, LANES), F32),
            pltpu.VMEM((8 * BLOCKS, LANES), F32),
            pltpu.SMEM((1, BLOCKS), jnp.int32),
            pltpu.SMEM((1, 2 * HALO), jnp.int32),
            pltpu.SemaphoreType.DMA((5,)),
        ],
        grant=GATHER_GRANT,
    )(jnp.transpose(x[0], (1, 0, 2)), jnp.transpose(v[0], (1, 0, 2)), masses[0], counts, picks_first)
    outer, inner = exchange(outer, inner)
    state, (new_slot, picks_second) = half_step(
        table, outer, inner, near_first, picks_first, (new_slot, picks_second)
    )
    stay, send = call(
        force_move_kernel,
        "force_move",
        (TABLE, shape(groups, MOVES, 8, LANES)),
        FORCE_SPECS + [HBM],
        FORCE_SCRATCH
        + [pltpu.SMEM((groups,), jnp.int32), pltpu.SMEM((1, BLOCKS), jnp.int32), pltpu.SemaphoreType.DMA],
    )(*state, new_slot)
    arrived = lax.all_to_all(send, "group", 0, 0)
    table, outer, inner = call(
        arrive_kernel,
        "arrive",
        (TABLE, LISTED, LISTED),
        [VMEM, VMEM, HBM],
        [pltpu.SMEM((1, 2 * HALO), jnp.int32), pltpu.SemaphoreType.DMA],
    )(stay, arrived, picks_second)
    outer, inner = exchange(outer, inner)
    state, _ = half_step(table, outer, inner, near_second, picks_second)
    x_out, v_out = call(
        force_out_kernel,
        "force_out",
        (shape(3, BLOCKS, LANES), shape(3, BLOCKS, LANES)),
        FORCE_SPECS,
        FORCE_SCRATCH + [pltpu.VMEM((8 * BLOCKS, LANES), F32)],
    )(*state)
    rho = state[1].reshape(1, BLOCKS, LANES)
    return jnp.transpose(x_out, (1, 0, 2))[None], jnp.transpose(v_out, (1, 0, 2))[None], rho


def solution(mesh):
    in_specs = (
        P("group", "curve", None, None),
        P("group", "curve", None, None),
        P("group", "curve", None),
        P("group", "curve"),
        P("group", "curve", None),
        P("group", "curve"),
        P("group", "curve"),
        P("group", "curve", None),
        P("group", "curve"),
    )
    out_specs = (
        P("group", "curve", None, None),
        P("group", "curve", None, None),
        P("group", "curve", None),
    )
    return jax.shard_map(body, mesh=mesh, in_specs=in_specs, out_specs=out_specs, check_vma=False)
```

```python
import math

import jax
import jax.numpy as jnp
from jax import lax
from jax.experimental import pallas as pl
from jax.experimental.pallas import tpu as pltpu
from jax.sharding import PartitionSpec as P


SOFTENING = 0.0025
BACKGROUND = 0.5
TIME_STEP = 0.1
SPACING = 0.6

BLOCKS = 16
HALO = 4
NBR = 6
CANDIDATES = BLOCKS + 2 * HALO
LANES = 128
FEATURES = 64
MOVES = 2
GATHER_GRANT = 63_000_000
KAPPA = 4.0 * math.log2(math.e)
MASS_SCALE = 2.0 ** (KAPPA * SOFTENING)
FORCE_SCALE = 8.0 * MASS_SCALE
NO_MASS = -4096.0

F32 = jnp.float32
BF16 = jnp.bfloat16
VMEM = pl.BlockSpec(memory_space=pltpu.VMEM)
SMEM = pl.BlockSpec(memory_space=pltpu.SMEM)
HBM = pl.BlockSpec(memory_space=pltpu.HBM)


def rounded(value):
    return value.astype(BF16).astype(F32)


def split(value):
    high = rounded(value)
    rest = value - high
    middle = rounded(rest)
    return high, middle, rest - middle


def tile_rows():
    return lax.broadcasted_iota(jnp.int32, (8, LANES), 0)


def three_rows(rows, first, parts):
    return jnp.where(
        rows == first, parts[0], jnp.where(rows == first + 1, parts[1], jnp.where(rows == first + 2, parts[2], 0.0))
    )


def local_tile(tile, base, rows):
    shifted = jnp.where(rows == 0, tile - base, tile)
    return jnp.where(rows < 6, shifted, 0.0)


def swapped(local, rows):
    down = pltpu.roll(local, 5, axis=0)
    up = pltpu.roll(local, 3, axis=0)
    return jnp.where(rows < 3, down, jnp.where(rows < 6, up, 0.0))


def quadratics(local, other, rows):
    square = jnp.sum(jnp.where(rows < 3, local * local, 0.0), axis=0, keepdims=True)
    mixed = jnp.sum(jnp.where(rows < 3, local * other, 0.0), axis=0, keepdims=True)
    return square, mixed


def target_features(tile, base, rows):
    local = local_tile(tile, base, rows)
    other = swapped(local, rows)
    square, mixed = quadratics(local, other, rows)
    near = split(jnp.where(rows < 3, (2.0 * KAPPA) * local, 0.0))
    flow = split(-KAPPA * other)
    minus = jnp.where(rows < 3, -1.0, 0.0)
    plus = jnp.where((rows >= 3) & (rows < 6), 1.0, 0.0)
    last_near = three_rows(rows, 0, split(-KAPPA * (square + SOFTENING)))
    last_flow = three_rows(rows, 0, split(KAPPA * mixed))
    near = [near[0], near[1], near[2], near[0], near[1], near[0]]
    flow = [flow[0], flow[1], flow[2], flow[0], flow[1], flow[0]]
    distance = jnp.concatenate(near + [minus, last_near], axis=0)
    approach = jnp.concatenate(flow + [plus, last_flow], axis=0)
    weighted = jnp.concatenate(
        near + [jnp.where(rows >= 6, 1.0, minus), jnp.where(rows == 3, 1.0, last_near)], axis=0
    )
    return distance.astype(BF16), approach.astype(BF16), weighted.astype(BF16)


def source_features(tile, base, rows):
    local = local_tile(tile, base, rows)
    other = swapped(local, rows)
    square, mixed = quadratics(local, other, rows)
    high, middle, low = split(local)
    mass = tile[6:7]
    alive = mass > 0.0
    exponent = jnp.where(alive, jnp.log2(jnp.where(alive, mass, 1.0)) + KAPPA * SOFTENING, NO_MASS)
    exponents = split(exponent)
    quadratic = three_rows(rows, 0, split(KAPPA * square)) + three_rows(rows, 3, split(KAPPA * mixed))
    quadratic = jnp.where(rows == 6, exponents[0], jnp.where(rows == 7, exponents[1], quadratic))
    ones = jnp.where(rows < 3, 1.0, jnp.where(rows == 3, exponents[2], 0.0))
    stacked = jnp.concatenate([high, high, high, middle, middle, low, quadratic, ones], axis=0)
    weights = split((mass * FORCE_SCALE) * jnp.where(rows < 3, local, jnp.where(rows == 3, 1.0, 0.0)))
    summed = jnp.concatenate([weights[0], weights[1], weights[2], jnp.zeros_like(local)], axis=0).astype(BF16)
    return stacked.T.astype(BF16), jnp.concatenate([summed, summed], axis=1)


def base_of_segment():
    return SPACING * lax.axis_index("curve").astype(F32)


def parity():
    return lax.rem(lax.axis_index("curve"), 2)


def list_blocks(table_ref, picks_ref, outer_ref, inner_ref):
    odd = parity()
    for h in range(HALO):
        outer_ref[h] = table_ref[picks_ref[0, odd * HALO + h]]
        inner_ref[h] = table_ref[picks_ref[0, (1 - odd) * HALO + h]]


def gather_kernel(
    x_hbm, v_hbm, m_hbm, counts_hbm, picks_hbm,
    table_ref, outer_ref, inner_ref,
    x_ref, v_ref, m_ref, flat_ref, counts_ref, picks_ref, sems,
):
    pairs = ((x_hbm, x_ref), (v_hbm, v_ref), (m_hbm, m_ref), (counts_hbm, counts_ref), (picks_hbm, picks_ref))
    copies = [pltpu.make_async_copy(source, target, sems.at[n]) for n, (source, target) in enumerate(pairs)]
    for copy in copies:
        copy.start()
    for copy in copies:
        copy.wait()
    for axis_id in range(3):
        flat_ref[pl.ds(axis_id, BLOCKS, stride=8), :] = x_ref[axis_id]
        flat_ref[pl.ds(3 + axis_id, BLOCKS, stride=8), :] = v_ref[axis_id]
    lane = lax.broadcasted_iota(jnp.int32, (1, LANES), 1)
    for b in range(BLOCKS):
        live = jnp.where(lane < counts_ref[0, b], m_ref[pl.ds(b, 1), :], 0.0)
        flat_ref[pl.ds(8 * b + 6, 1), :] = live
        flat_ref[pl.ds(8 * b + 7, 1), :] = jnp.zeros_like(live)
    for b in range(BLOCKS):
        table_ref[b] = flat_ref[pl.ds(8 * b, 8), :]
    list_blocks(table_ref, picks_ref, outer_ref, inner_ref)


def features_kernel(table_ref, *refs):
    target_ref, source_ref, sum_ref = refs[-3:]
    passed = (len(refs) - 3) // 2
    for n in range(passed):
        refs[passed + n][...] = refs[n][...]
    base = base_of_segment()
    rows = tile_rows()

    def own(b, carry):
        tile = table_ref[b]
        source_ref[b], sum_ref[b] = source_features(tile, base, rows)
        parts = target_features(tile, base, rows)
        for n in range(3):
            target_ref[b, :, n * LANES : (n + 1) * LANES] = parts[n]
        return carry

    lax.fori_loop(0, BLOCKS, own, 0, unroll=4)


def density_of(j, target_ref, source_ref, near_ref):
    right = target_ref[j, :, 2 * LANES : 3 * LANES]
    sources = [j] + [near_ref[n, 0, j] for n in range(NBR)]
    left = jnp.concatenate([source_ref[s] for s in sources], axis=0)
    weight = jnp.exp2(jnp.dot(left, right, preferred_element_type=F32))
    return BACKGROUND + jnp.sum(weight, axis=0, keepdims=True)


def listed_density_kernel(
    outer_ref, inner_ref, near_ref, picks_ref, target_ref, own_source_ref, own_sum_ref,
    outer_out_ref, source_ref, sum_ref,
):
    base = base_of_segment()
    odd = parity()
    rows = tile_rows()
    for b in range(BLOCKS):
        source_ref[b] = own_source_ref[b]
        sum_ref[b] = own_sum_ref[b]
    for h in range(HALO):
        for block_ref, side in ((outer_ref, odd), (inner_ref, 1 - odd)):
            at = BLOCKS + side * HALO + h
            source_ref[at], sum_ref[at] = source_features(block_ref[h], base, rows)

    for h in range(HALO):
        j = picks_ref[0, odd * HALO + h]
        outer_out_ref[pl.ds(h, 1), :] = density_of(j, target_ref, source_ref, near_ref)


def density_kernel(near_ref, picks_ref, target_ref, source_ref, rho_ref, inner_out_ref):
    odd = parity()

    def target(j, carry):
        rho_ref[j] = density_of(j, target_ref, source_ref, near_ref)
        return carry

    lax.fori_loop(0, BLOCKS, target, 0, unroll=2)
    for h in range(HALO):
        inner_out_ref[pl.ds(h, 1), :] = rho_ref[picks_ref[0, (1 - odd) * HALO + h]]


def advance(
    table_ref, rho_ref, outer_ref, inner_ref, near_ref, target_ref, source_ref, sum_ref, rho_of, inverse_of, done
):
    base = base_of_segment()
    rows = tile_rows()
    even = parity() == 0
    outer, inner = outer_ref[...], inner_ref[...]
    below = jnp.where(even, outer, inner)
    above = jnp.where(even, inner, outer)
    flat = [rho_ref[b] for b in range(BLOCKS)] + [below, above, jnp.ones((8, LANES), F32)]
    flat = jnp.concatenate(flat, axis=0)
    across = flat.T
    for s in range(CANDIDATES):
        column = jnp.broadcast_to(across[:, s : s + 1], (LANES, LANES))
        rho_of[s] = column
        inverse_of[s] = 1.0 / column

    def target(j, carry):
        right = target_ref[j, :, 0 : 2 * LANES]
        mine = rho_ref[j]
        mine_inverse = 1.0 / mine
        sources = [j] + [near_ref[n, 0, j] for n in range(NBR)]
        wholes, lefts = [], []
        for s in sources:
            product = jnp.dot(source_ref[s], right, preferred_element_type=F32)
            distance = product[:, 0:LANES]
            approach = product[:, LANES : 2 * LANES]
            closing = jnp.minimum(approach, 0.0) / (distance * (mine + rho_of[s]))
            factor = jnp.exp2(distance) * (closing + (mine_inverse + inverse_of[s]))
            high = factor.astype(BF16)
            low = (factor - high.astype(F32)).astype(BF16)
            wholes += [high, low]
            lefts.append(sum_ref[s])
        total = jnp.dot(jnp.concatenate(lefts, axis=1), jnp.concatenate(wholes, axis=0), preferred_element_type=F32)
        sums = total[0:8] + total[8:16] + total[16:24]
        tile = table_ref[j]
        local = local_tile(tile, base, rows)
        accel = jnp.where(rows < 3, local * sums[3:4] - sums, 0.0)
        kicked = tile + TIME_STEP * pltpu.roll(accel, 3, axis=0)
        drift = pltpu.roll(kicked, 5, axis=0)
        done(j, jnp.where(rows < 3, kicked + TIME_STEP * drift, kicked))
        return carry

    lax.fori_loop(0, BLOCKS, target, 0, unroll=2)


def force_move_kernel(
    table_ref, rho_ref, outer_ref, inner_ref, near_ref, target_ref, source_ref, sum_ref, slot_hbm,
    stay_ref, send_ref, rho_of, inverse_of, filled, slot_ref, sem, moved_ref,
):
    copy = pltpu.make_async_copy(slot_hbm, slot_ref, sem)
    copy.start()
    me = lax.axis_index("group")
    rows = tile_rows()
    groups = send_ref.shape[0]
    for g in range(groups):
        filled[g] = 0
        for k in range(MOVES):
            send_ref[g, k] = jnp.full((8, LANES), -1.0, F32)
    for b in range(BLOCKS):
        stay_ref[b] = jnp.zeros((8, LANES), F32)
    copy.wait()

    def done(b, tile):
        moved_ref[b] = tile

    advance(
        table_ref, rho_ref, outer_ref, inner_ref, near_ref, target_ref, source_ref, sum_ref, rho_of, inverse_of, done
    )

    def route(b, carry):
        owner = slot_ref[0, b] // BLOCKS
        slot = slot_ref[0, b] % BLOCKS
        tagged = jnp.where(rows == 7, jnp.full((8, LANES), slot, jnp.int32).astype(F32), moved_ref[b])

        @pl.when(owner == me)
        def _():
            stay_ref[slot] = tagged

        @pl.when(owner != me)
        def _():
            place = jnp.minimum(filled[owner], MOVES - 1)
            send_ref[owner, place] = tagged
            filled[owner] = place + 1

        return carry

    lax.fori_loop(0, BLOCKS, route, 0)


def arrive_kernel(stay_ref, arrived_ref, picks_hbm, table_ref, outer_ref, inner_ref, picks_ref, sem):
    copy = pltpu.make_async_copy(picks_hbm, picks_ref, sem)
    copy.start()
    groups = arrived_ref.shape[0]
    tiles = [arrived_ref[g, k] for g in range(groups) for k in range(MOVES)]
    tags = [jnp.broadcast_to(tile[7:8], (8, LANES)) for tile in tiles]
    for s in range(BLOCKS):
        value = stay_ref[s]
        for tile, tag in zip(tiles, tags):
            value = jnp.where(tag == float(s), tile, value)
        table_ref[s] = value
    copy.wait()
    list_blocks(table_ref, picks_ref, outer_ref, inner_ref)


def force_out_kernel(
    table_ref, rho_ref, outer_ref, inner_ref, near_ref, target_ref, source_ref, sum_ref,
    x_ref, v_ref, rho_out_ref, rho_of, inverse_of, flat_ref,
):
    def done(b, tile):
        flat_ref[pl.ds(pl.multiple_of(8 * b, 8), 8), :] = tile

    advance(
        table_ref, rho_ref, outer_ref, inner_ref, near_ref, target_ref, source_ref, sum_ref, rho_of, inverse_of, done
    )
    for b in range(BLOCKS):
        rho_out_ref[pl.ds(b, 1), :] = rho_ref[b]
    for axis_id in range(3):
        x_ref[axis_id] = flat_ref[pl.ds(axis_id, BLOCKS, stride=8), :]
        v_ref[axis_id] = flat_ref[pl.ds(3 + axis_id, BLOCKS, stride=8), :]


def shape(*dims, dtype=F32):
    return jax.ShapeDtypeStruct(dims, dtype)


TABLE = shape(BLOCKS, 8, LANES)
LISTED = shape(HALO, 8, LANES)


def call(kernel, out_shape, in_specs, scratch=(), flops=0, grant=16 << 20):
    return pl.pallas_call(
        kernel,
        out_shape=out_shape,
        in_specs=in_specs,
        out_specs=[VMEM] * len(out_shape),
        scratch_shapes=list(scratch),
        cost_estimate=pl.CostEstimate(flops=flops, bytes_accessed=200000, transcendentals=0),
        compiler_params=pltpu.CompilerParams(vmem_limit_bytes=grant),
    )


def swap_outer(item):
    count = lax.axis_size("curve")
    pairs = [(i, (i + 1) % count) for i in range(1, count, 2)]
    return lax.ppermute(item, "curve", pairs + [(target, source) for source, target in pairs])


def swap_inner(item):
    pairs = [(i, i + 1) for i in range(0, lax.axis_size("curve"), 2)]
    return lax.ppermute(item, "curve", pairs + [(target, source) for source, target in pairs])


SOURCES = (
    shape(CANDIDATES, LANES, FEATURES, dtype=BF16),
    shape(CANDIDATES, 32, 2 * LANES, dtype=BF16),
)
OWN_SOURCES = (
    shape(BLOCKS, LANES, FEATURES, dtype=BF16),
    shape(BLOCKS, 32, 2 * LANES, dtype=BF16),
)


def half_step(table, outer, inner, near, picks, passed=()):
    outer = swap_outer(outer)
    inner = swap_inner(inner)
    passed = (near, picks) + tuple(passed)
    near, picks, *passed, targets, own_source, own_sum = call(
        features_kernel,
        tuple(shape(*item.shape, dtype=item.dtype) for item in passed)
        + (shape(BLOCKS, FEATURES, 3 * LANES, dtype=BF16),)
        + OWN_SOURCES,
        [VMEM] * (1 + len(passed)),
    )(table, *passed)
    outer_rho, sources, sums = call(
        listed_density_kernel, (shape(HALO, LANES),) + SOURCES, [VMEM, VMEM, SMEM, SMEM, VMEM, VMEM, VMEM]
    )(outer, inner, near, picks, targets, own_source, own_sum)
    outer_rho = swap_outer(outer_rho)
    rho, inner_rho = call(
        density_kernel, (shape(BLOCKS, 1, LANES), shape(HALO, LANES)), [SMEM, SMEM, VMEM, VMEM]
    )(near, picks, targets, sources)
    inner_rho = swap_inner(inner_rho)
    return (table, rho, outer_rho, inner_rho, near, targets, sources, sums), passed


FORCE_SPECS = [VMEM, VMEM, VMEM, VMEM, SMEM, VMEM, VMEM, VMEM]
FORCE_SCRATCH = [pltpu.VMEM((CANDIDATES, LANES, LANES), F32)] * 2


def body(x, v, masses, counts, near_first, picks_first, new_slot, near_second, picks_second):
    groups = lax.axis_size("group")
    near_first = jnp.transpose(near_first, (2, 0, 1))
    near_second = jnp.transpose(near_second, (2, 0, 1))
    table, outer, inner = call(
        gather_kernel,
        (TABLE, LISTED, LISTED),
        [HBM] * 5,
        [
            pltpu.VMEM((3, BLOCKS, LANES), F32),
            pltpu.VMEM((3, BLOCKS, LANES), F32),
            pltpu.VMEM((BLOCKS, LANES), F32),
            pltpu.VMEM((8 * BLOCKS, LANES), F32),
            pltpu.SMEM((1, BLOCKS), jnp.int32),
            pltpu.SMEM((1, 2 * HALO), jnp.int32),
            pltpu.SemaphoreType.DMA((5,)),
        ],
        grant=GATHER_GRANT,
    )(jnp.transpose(x[0], (1, 0, 2)), jnp.transpose(v[0], (1, 0, 2)), masses[0], counts, picks_first)
    state, (new_slot, picks_second) = half_step(table, outer, inner, near_first, picks_first, (new_slot, picks_second))
    stay, send = call(
        force_move_kernel,
        (TABLE, shape(groups, MOVES, 8, LANES)),
        FORCE_SPECS + [HBM],
        FORCE_SCRATCH
        + [pltpu.SMEM((groups,), jnp.int32), pltpu.SMEM((1, BLOCKS), jnp.int32), pltpu.SemaphoreType.DMA]
        + [pltpu.VMEM((BLOCKS, 8, LANES), F32)],
    )(*state, new_slot)
    arrived = lax.all_to_all(send, "group", 0, 0)
    table, outer, inner = call(
        arrive_kernel,
        (TABLE, LISTED, LISTED),
        [VMEM, VMEM, HBM],
        [pltpu.SMEM((1, 2 * HALO), jnp.int32), pltpu.SemaphoreType.DMA],
    )(stay, arrived, picks_second)
    state, _ = half_step(table, outer, inner, near_second, picks_second)
    x_out, v_out, rho = call(
        force_out_kernel,
        (shape(3, BLOCKS, LANES), shape(3, BLOCKS, LANES), shape(BLOCKS, LANES)),
        FORCE_SPECS,
        FORCE_SCRATCH + [pltpu.VMEM((8 * BLOCKS, LANES), F32)],
    )(*state)
    return jnp.transpose(x_out, (1, 0, 2))[None], jnp.transpose(v_out, (1, 0, 2))[None], rho[None]


def solution(mesh):
    in_specs = (
        P("group", "curve", None, None),
        P("group", "curve", None, None),
        P("group", "curve", None),
        P("group", "curve"),
        P("group", "curve", None),
        P("group", "curve"),
        P("group", "curve"),
        P("group", "curve", None),
        P("group", "curve"),
    )
    out_specs = (
        P("group", "curve", None, None),
        P("group", "curve", None, None),
        P("group", "curve", None),
    )
    return jax.shard_map(body, mesh=mesh, in_specs=in_specs, out_specs=out_specs, check_vma=False)
```

```python
import math

import jax
import jax.numpy as jnp
from jax import lax
from jax.experimental import pallas as pl
from jax.experimental.pallas import tpu as pltpu
from jax.sharding import PartitionSpec as P


SOFTENING = 0.0025
BACKGROUND = 0.5
TIME_STEP = 0.1
SPACING = 0.6

BLOCKS = 16
HALO = 4
NBR = 6
CANDIDATES = BLOCKS + 2 * HALO
LANES = 128
FEATURES = 64
MOVES = 2
GATHER_GRANT = 63_000_000
KAPPA = 4.0 * math.log2(math.e)
MASS_SCALE = 2.0 ** (KAPPA * SOFTENING)
FORCE_SCALE = 8.0 * MASS_SCALE
NO_MASS = -4096.0

F32 = jnp.float32
BF16 = jnp.bfloat16
VMEM = pl.BlockSpec(memory_space=pltpu.VMEM)
SMEM = pl.BlockSpec(memory_space=pltpu.SMEM)
HBM = pl.BlockSpec(memory_space=pltpu.HBM)


def rounded(value):
    return value.astype(BF16).astype(F32)


def split(value):
    high = rounded(value)
    rest = value - high
    middle = rounded(rest)
    return high, middle, rest - middle


def tile_rows():
    return lax.broadcasted_iota(jnp.int32, (8, LANES), 0)


def three_rows(rows, first, parts):
    return jnp.where(
        rows == first, parts[0], jnp.where(rows == first + 1, parts[1], jnp.where(rows == first + 2, parts[2], 0.0))
    )


def local_tile(tile, base, rows):
    shifted = jnp.where(rows == 0, tile - base, tile)
    return jnp.where(rows < 6, shifted, 0.0)


def swapped(local, rows):
    down = pltpu.roll(local, 5, axis=0)
    up = pltpu.roll(local, 3, axis=0)
    return jnp.where(rows < 3, down, jnp.where(rows < 6, up, 0.0))


def quadratics(local, other, rows):
    square = jnp.sum(jnp.where(rows < 3, local * local, 0.0), axis=0, keepdims=True)
    mixed = jnp.sum(jnp.where(rows < 3, local * other, 0.0), axis=0, keepdims=True)
    return square, mixed


def target_features(tile, base, rows):
    local = local_tile(tile, base, rows)
    other = swapped(local, rows)
    square, mixed = quadratics(local, other, rows)
    near = split(jnp.where(rows < 3, (2.0 * KAPPA) * local, 0.0))
    flow = split(-KAPPA * other)
    minus = jnp.where(rows < 3, -1.0, 0.0)
    plus = jnp.where((rows >= 3) & (rows < 6), 1.0, 0.0)
    last_near = three_rows(rows, 0, split(-KAPPA * (square + SOFTENING)))
    last_flow = three_rows(rows, 0, split(KAPPA * mixed))
    near = [near[0], near[1], near[2], near[0], near[1], near[0]]
    flow = [flow[0], flow[1], flow[2], flow[0], flow[1], flow[0]]
    distance = jnp.concatenate(near + [minus, last_near], axis=0)
    approach = jnp.concatenate(flow + [plus, last_flow], axis=0)
    weighted = jnp.concatenate(
        near + [jnp.where(rows >= 6, 1.0, minus), jnp.where(rows == 3, 1.0, last_near)], axis=0
    )
    return distance.astype(BF16), approach.astype(BF16), weighted.astype(BF16)


def source_features(tile, base, rows):
    local = local_tile(tile, base, rows)
    other = swapped(local, rows)
    square, mixed = quadratics(local, other, rows)
    high, middle, low = split(local)
    mass = tile[6:7]
    alive = mass > 0.0
    exponent = jnp.where(alive, jnp.log2(jnp.where(alive, mass, 1.0)) + KAPPA * SOFTENING, NO_MASS)
    exponents = split(exponent)
    quadratic = three_rows(rows, 0, split(KAPPA * square)) + three_rows(rows, 3, split(KAPPA * mixed))
    quadratic = jnp.where(rows == 6, exponents[0], jnp.where(rows == 7, exponents[1], quadratic))
    ones = jnp.where(rows < 3, 1.0, jnp.where(rows == 3, exponents[2], 0.0))
    stacked = jnp.concatenate([high, high, high, middle, middle, low, quadratic, ones], axis=0)
    weights = split((mass * FORCE_SCALE) * jnp.where(rows < 3, local, jnp.where(rows == 3, 1.0, 0.0)))
    summed = jnp.concatenate([weights[0], weights[1], weights[2], jnp.zeros_like(local)], axis=0).astype(BF16)
    return stacked.T.astype(BF16), jnp.concatenate([summed, summed], axis=1)


def base_of_segment():
    return SPACING * lax.axis_index("curve").astype(F32)


def parity():
    return lax.rem(lax.axis_index("curve"), 2)


def list_blocks(table_ref, picks_ref, outer_ref, inner_ref):
    odd = parity()
    for h in range(HALO):
        outer_ref[h] = table_ref[picks_ref[0, odd * HALO + h]]
        inner_ref[h] = table_ref[picks_ref[0, (1 - odd) * HALO + h]]


def gather_kernel(
    x_hbm, v_hbm, m_hbm, counts_hbm, picks_hbm,
    table_ref, outer_ref, inner_ref,
    x_ref, v_ref, m_ref, flat_ref, counts_ref, picks_ref, sems,
):
    pairs = ((x_hbm, x_ref), (v_hbm, v_ref), (m_hbm, m_ref), (counts_hbm, counts_ref), (picks_hbm, picks_ref))
    copies = [pltpu.make_async_copy(source, target, sems.at[n]) for n, (source, target) in enumerate(pairs)]
    for copy in copies:
        copy.start()
    for copy in copies:
        copy.wait()
    for axis_id in range(3):
        flat_ref[pl.ds(axis_id, BLOCKS, stride=8), :] = x_ref[axis_id]
        flat_ref[pl.ds(3 + axis_id, BLOCKS, stride=8), :] = v_ref[axis_id]
    lane = lax.broadcasted_iota(jnp.int32, (1, LANES), 1)
    for b in range(BLOCKS):
        live = jnp.where(lane < counts_ref[0, b], m_ref[pl.ds(b, 1), :], 0.0)
        flat_ref[pl.ds(8 * b + 6, 1), :] = live
        flat_ref[pl.ds(8 * b + 7, 1), :] = jnp.zeros_like(live)
    for b in range(BLOCKS):
        table_ref[b] = flat_ref[pl.ds(8 * b, 8), :]
    list_blocks(table_ref, picks_ref, outer_ref, inner_ref)


def features_kernel(table_ref, *refs):
    target_ref, source_ref, sum_ref = refs[-3:]
    passed = (len(refs) - 3) // 2
    for n in range(passed):
        refs[passed + n][...] = refs[n][...]
    base = base_of_segment()
    rows = tile_rows()

    def own(b, carry):
        tile = table_ref[b]
        source_ref[b], sum_ref[b] = source_features(tile, base, rows)
        parts = target_features(tile, base, rows)
        for n in range(3):
            target_ref[b, :, n * LANES : (n + 1) * LANES] = parts[n]
        return carry

    lax.fori_loop(0, BLOCKS, own, 0, unroll=4)


def density_of(j, target_ref, source_ref, near_ref):
    right = target_ref[j, :, 2 * LANES : 3 * LANES]
    sources = [j] + [near_ref[n, 0, j] for n in range(NBR)]
    left = jnp.concatenate([source_ref[s] for s in sources], axis=0)
    weight = jnp.exp2(jnp.dot(left, right, preferred_element_type=F32))
    return BACKGROUND + jnp.sum(weight, axis=0, keepdims=True)


def listed_density_kernel(
    outer_ref, inner_ref, near_ref, picks_ref, target_ref, own_source_ref, own_sum_ref,
    outer_out_ref, inner_out_ref, source_ref, sum_ref,
):
    base = base_of_segment()
    odd = parity()
    rows = tile_rows()
    for b in range(BLOCKS):
        source_ref[b] = own_source_ref[b]
        sum_ref[b] = own_sum_ref[b]
    for h in range(HALO):
        for block_ref, side in ((outer_ref, odd), (inner_ref, 1 - odd)):
            at = BLOCKS + side * HALO + h
            source_ref[at], sum_ref[at] = source_features(block_ref[h], base, rows)

    for out_ref, side in ((outer_out_ref, odd), (inner_out_ref, 1 - odd)):
        for h in range(HALO):
            j = picks_ref[0, side * HALO + h]
            out_ref[pl.ds(h, 1), :] = density_of(j, target_ref, source_ref, near_ref)


def density_kernel(near_ref, target_ref, source_ref, rho_ref):
    def target(j, carry):
        rho_ref[j] = density_of(j, target_ref, source_ref, near_ref)
        return carry

    lax.fori_loop(0, BLOCKS, target, 0, unroll=2)


def advance(
    table_ref, rho_ref, outer_ref, inner_ref, near_ref, target_ref, source_ref, sum_ref, rho_of, inverse_of, done
):
    base = base_of_segment()
    rows = tile_rows()
    even = parity() == 0
    outer, inner = outer_ref[...], inner_ref[...]
    below = jnp.where(even, outer, inner)
    above = jnp.where(even, inner, outer)
    flat = [rho_ref[b] for b in range(BLOCKS)] + [below, above, jnp.ones((8, LANES), F32)]
    flat = jnp.concatenate(flat, axis=0)
    across = flat.T
    for s in range(CANDIDATES):
        column = jnp.broadcast_to(across[:, s : s + 1], (LANES, LANES))
        rho_of[s] = column
        inverse_of[s] = 1.0 / column

    def target(j, carry):
        right = target_ref[j, :, 0 : 2 * LANES]
        mine = rho_ref[j]
        mine_inverse = 1.0 / mine
        sources = [j] + [near_ref[n, 0, j] for n in range(NBR)]
        wholes, lefts = [], []
        for s in sources:
            product = jnp.dot(source_ref[s], right, preferred_element_type=F32)
            distance = product[:, 0:LANES]
            approach = product[:, LANES : 2 * LANES]
            closing = jnp.minimum(approach, 0.0) / (distance * (mine + rho_of[s]))
            factor = jnp.exp2(distance) * (closing + (mine_inverse + inverse_of[s]))
            high = factor.astype(BF16)
            low = (factor - high.astype(F32)).astype(BF16)
            wholes += [high, low]
            lefts.append(sum_ref[s])
        total = jnp.dot(jnp.concatenate(lefts, axis=1), jnp.concatenate(wholes, axis=0), preferred_element_type=F32)
        sums = total[0:8] + total[8:16] + total[16:24]
        tile = table_ref[j]
        local = local_tile(tile, base, rows)
        accel = jnp.where(rows < 3, local * sums[3:4] - sums, 0.0)
        kicked = tile + TIME_STEP * pltpu.roll(accel, 3, axis=0)
        drift = pltpu.roll(kicked, 5, axis=0)
        done(j, jnp.where(rows < 3, kicked + TIME_STEP * drift, kicked))
        return carry

    lax.fori_loop(0, BLOCKS, target, 0, unroll=2)


def force_move_kernel(
    table_ref, rho_ref, outer_ref, inner_ref, near_ref, target_ref, source_ref, sum_ref, slot_hbm,
    stay_ref, send_ref, rho_of, inverse_of, filled, slot_ref, sem, moved_ref,
):
    copy = pltpu.make_async_copy(slot_hbm, slot_ref, sem)
    copy.start()
    me = lax.axis_index("group")
    rows = tile_rows()
    groups = send_ref.shape[0]
    for g in range(groups):
        filled[g] = 0
        for k in range(MOVES):
            send_ref[g, k] = jnp.full((8, LANES), -1.0, F32)
    for b in range(BLOCKS):
        stay_ref[b] = jnp.zeros((8, LANES), F32)
    copy.wait()

    def done(b, tile):
        moved_ref[b] = tile

    advance(
        table_ref, rho_ref, outer_ref, inner_ref, near_ref, target_ref, source_ref, sum_ref, rho_of, inverse_of, done
    )

    def route(b, carry):
        owner = slot_ref[0, b] // BLOCKS
        slot = slot_ref[0, b] % BLOCKS
        tagged = jnp.where(rows == 7, jnp.full((8, LANES), slot, jnp.int32).astype(F32), moved_ref[b])

        @pl.when(owner == me)
        def _():
            stay_ref[slot] = tagged

        @pl.when(owner != me)
        def _():
            place = jnp.minimum(filled[owner], MOVES - 1)
            send_ref[owner, place] = tagged
            filled[owner] = place + 1

        return carry

    lax.fori_loop(0, BLOCKS, route, 0)


def arrive_kernel(stay_ref, arrived_ref, picks_hbm, table_ref, outer_ref, inner_ref, picks_ref, sem):
    copy = pltpu.make_async_copy(picks_hbm, picks_ref, sem)
    copy.start()
    groups = arrived_ref.shape[0]
    tiles = [arrived_ref[g, k] for g in range(groups) for k in range(MOVES)]
    tags = [jnp.broadcast_to(tile[7:8], (8, LANES)) for tile in tiles]
    for s in range(BLOCKS):
        value = stay_ref[s]
        for tile, tag in zip(tiles, tags):
            value = jnp.where(tag == float(s), tile, value)
        table_ref[s] = value
    copy.wait()
    list_blocks(table_ref, picks_ref, outer_ref, inner_ref)


def force_out_kernel(
    table_ref, rho_ref, outer_ref, inner_ref, near_ref, target_ref, source_ref, sum_ref,
    x_ref, v_ref, rho_out_ref, rho_of, inverse_of, flat_ref,
):
    def done(b, tile):
        flat_ref[pl.ds(pl.multiple_of(8 * b, 8), 8), :] = tile

    advance(
        table_ref, rho_ref, outer_ref, inner_ref, near_ref, target_ref, source_ref, sum_ref, rho_of, inverse_of, done
    )
    for b in range(BLOCKS):
        rho_out_ref[pl.ds(b, 1), :] = rho_ref[b]
    for axis_id in range(3):
        x_ref[axis_id] = flat_ref[pl.ds(axis_id, BLOCKS, stride=8), :]
        v_ref[axis_id] = flat_ref[pl.ds(3 + axis_id, BLOCKS, stride=8), :]


def shape(*dims, dtype=F32):
    return jax.ShapeDtypeStruct(dims, dtype)


TABLE = shape(BLOCKS, 8, LANES)
LISTED = shape(HALO, 8, LANES)


def call(kernel, out_shape, in_specs, scratch=(), flops=0, grant=16 << 20):
    return pl.pallas_call(
        kernel,
        out_shape=out_shape,
        in_specs=in_specs,
        out_specs=[VMEM] * len(out_shape),
        scratch_shapes=list(scratch),
        cost_estimate=pl.CostEstimate(flops=flops, bytes_accessed=200000, transcendentals=0),
        compiler_params=pltpu.CompilerParams(vmem_limit_bytes=grant),
    )


def swap_outer(item):
    count = lax.axis_size("curve")
    pairs = [(i, (i + 1) % count) for i in range(1, count, 2)]
    return lax.ppermute(item, "curve", pairs + [(target, source) for source, target in pairs])


def swap_inner(item):
    pairs = [(i, i + 1) for i in range(0, lax.axis_size("curve"), 2)]
    return lax.ppermute(item, "curve", pairs + [(target, source) for source, target in pairs])


SOURCES = (
    shape(CANDIDATES, LANES, FEATURES, dtype=BF16),
    shape(CANDIDATES, 32, 2 * LANES, dtype=BF16),
)
OWN_SOURCES = (
    shape(BLOCKS, LANES, FEATURES, dtype=BF16),
    shape(BLOCKS, 32, 2 * LANES, dtype=BF16),
)


def half_step(table, outer, inner, near, picks, passed=()):
    outer = swap_outer(outer)
    inner = swap_inner(inner)
    passed = (near, picks) + tuple(passed)
    near, picks, *passed, targets, own_source, own_sum = call(
        features_kernel,
        tuple(shape(*item.shape, dtype=item.dtype) for item in passed)
        + (shape(BLOCKS, FEATURES, 3 * LANES, dtype=BF16),)
        + OWN_SOURCES,
        [VMEM] * (1 + len(passed)),
    )(table, *passed)
    outer_rho, inner_rho, sources, sums = call(
        listed_density_kernel,
        (shape(HALO, LANES), shape(HALO, LANES)) + SOURCES,
        [VMEM, VMEM, SMEM, SMEM, VMEM, VMEM, VMEM],
    )(outer, inner, near, picks, targets, own_source, own_sum)
    outer_rho = swap_outer(outer_rho)
    inner_rho = swap_inner(inner_rho)
    (rho,) = call(density_kernel, (shape(BLOCKS, 1, LANES),), [SMEM, VMEM, VMEM])(near, targets, sources)
    return (table, rho, outer_rho, inner_rho, near, targets, sources, sums), passed


FORCE_SPECS = [VMEM, VMEM, VMEM, VMEM, SMEM, VMEM, VMEM, VMEM]
FORCE_SCRATCH = [pltpu.VMEM((CANDIDATES, LANES, LANES), F32)] * 2


def body(x, v, masses, counts, near_first, picks_first, new_slot, near_second, picks_second):
    groups = lax.axis_size("group")
    near_first = jnp.transpose(near_first, (2, 0, 1))
    near_second = jnp.transpose(near_second, (2, 0, 1))
    table, outer, inner = call(
        gather_kernel,
        (TABLE, LISTED, LISTED),
        [HBM] * 5,
        [
            pltpu.VMEM((3, BLOCKS, LANES), F32),
            pltpu.VMEM((3, BLOCKS, LANES), F32),
            pltpu.VMEM((BLOCKS, LANES), F32),
            pltpu.VMEM((8 * BLOCKS, LANES), F32),
            pltpu.SMEM((1, BLOCKS), jnp.int32),
            pltpu.SMEM((1, 2 * HALO), jnp.int32),
            pltpu.SemaphoreType.DMA((5,)),
        ],
        grant=GATHER_GRANT,
    )(jnp.transpose(x[0], (1, 0, 2)), jnp.transpose(v[0], (1, 0, 2)), masses[0], counts, picks_first)
    state, (new_slot, picks_second) = half_step(table, outer, inner, near_first, picks_first, (new_slot, picks_second))
    stay, send = call(
        force_move_kernel,
        (TABLE, shape(groups, MOVES, 8, LANES)),
        FORCE_SPECS + [HBM],
        FORCE_SCRATCH
        + [pltpu.SMEM((groups,), jnp.int32), pltpu.SMEM((1, BLOCKS), jnp.int32), pltpu.SemaphoreType.DMA]
        + [pltpu.VMEM((BLOCKS, 8, LANES), F32)],
    )(*state, new_slot)
    arrived = lax.all_to_all(send, "group", 0, 0)
    table, outer, inner = call(
        arrive_kernel,
        (TABLE, LISTED, LISTED),
        [VMEM, VMEM, HBM],
        [pltpu.SMEM((1, 2 * HALO), jnp.int32), pltpu.SemaphoreType.DMA],
    )(stay, arrived, picks_second)
    state, _ = half_step(table, outer, inner, near_second, picks_second)
    x_out, v_out, rho = call(
        force_out_kernel,
        (shape(3, BLOCKS, LANES), shape(3, BLOCKS, LANES), shape(BLOCKS, LANES)),
        FORCE_SPECS,
        FORCE_SCRATCH + [pltpu.VMEM((8 * BLOCKS, LANES), F32)],
    )(*state)
    return jnp.transpose(x_out, (1, 0, 2))[None], jnp.transpose(v_out, (1, 0, 2))[None], rho[None]


def solution(mesh):
    in_specs = (
        P("group", "curve", None, None),
        P("group", "curve", None, None),
        P("group", "curve", None),
        P("group", "curve"),
        P("group", "curve", None),
        P("group", "curve"),
        P("group", "curve"),
        P("group", "curve", None),
        P("group", "curve"),
    )
    out_specs = (
        P("group", "curve", None, None),
        P("group", "curve", None, None),
        P("group", "curve", None),
    )
    return jax.shard_map(body, mesh=mesh, in_specs=in_specs, out_specs=out_specs, check_vma=False)
```

```python
import math

import jax
import jax.numpy as jnp
from jax import lax
from jax.experimental import pallas as pl
from jax.experimental.pallas import tpu as pltpu
from jax.sharding import PartitionSpec as P


SOFTENING = 0.0025
BACKGROUND = 0.5
TIME_STEP = 0.1
SPACING = 0.6

BLOCKS = 16
HALO = 4
NBR = 6
CANDIDATES = BLOCKS + 2 * HALO
LANES = 128
FEATURES = 64
MOVES = 2
GATHER_GRANT = 63_000_000
KAPPA = 4.0 * math.log2(math.e)
MASS_SCALE = 2.0 ** (KAPPA * SOFTENING)
FORCE_SCALE = 8.0 * MASS_SCALE
NO_MASS = -4096.0

F32 = jnp.float32
BF16 = jnp.bfloat16
VMEM = pl.BlockSpec(memory_space=pltpu.VMEM)
SMEM = pl.BlockSpec(memory_space=pltpu.SMEM)
HBM = pl.BlockSpec(memory_space=pltpu.HBM)


def rounded(value):
    return value.astype(BF16).astype(F32)


def split(value):
    high = rounded(value)
    rest = value - high
    middle = rounded(rest)
    return high, middle, rest - middle


def tile_rows():
    return lax.broadcasted_iota(jnp.int32, (8, LANES), 0)


def three_rows(rows, first, parts):
    return jnp.where(
        rows == first, parts[0], jnp.where(rows == first + 1, parts[1], jnp.where(rows == first + 2, parts[2], 0.0))
    )


def local_tile(tile, base, rows):
    shifted = jnp.where(rows == 0, tile - base, tile)
    return jnp.where(rows < 6, shifted, 0.0)


def swapped(local, rows):
    down = pltpu.roll(local, 5, axis=0)
    up = pltpu.roll(local, 3, axis=0)
    return jnp.where(rows < 3, down, jnp.where(rows < 6, up, 0.0))


def quadratics(local, other, rows):
    square = jnp.sum(jnp.where(rows < 3, local * local, 0.0), axis=0, keepdims=True)
    mixed = jnp.sum(jnp.where(rows < 3, local * other, 0.0), axis=0, keepdims=True)
    return square, mixed


def target_features(tile, base, rows):
    local = local_tile(tile, base, rows)
    other = swapped(local, rows)
    square, mixed = quadratics(local, other, rows)
    near = split(jnp.where(rows < 3, (2.0 * KAPPA) * local, 0.0))
    flow = split(-KAPPA * other)
    minus = jnp.where(rows < 3, -1.0, 0.0)
    plus = jnp.where((rows >= 3) & (rows < 6), 1.0, 0.0)
    last_near = three_rows(rows, 0, split(-KAPPA * (square + SOFTENING)))
    last_flow = three_rows(rows, 0, split(KAPPA * mixed))
    near = [near[0], near[1], near[2], near[0], near[1], near[0]]
    flow = [flow[0], flow[1], flow[2], flow[0], flow[1], flow[0]]
    distance = jnp.concatenate(near + [minus, last_near], axis=0)
    approach = jnp.concatenate(flow + [plus, last_flow], axis=0)
    weighted = jnp.concatenate(
        near + [jnp.where(rows >= 6, 1.0, minus), jnp.where(rows == 3, 1.0, last_near)], axis=0
    )
    return distance.astype(BF16), approach.astype(BF16), weighted.astype(BF16)


def source_features(tile, base, rows):
    local = local_tile(tile, base, rows)
    other = swapped(local, rows)
    square, mixed = quadratics(local, other, rows)
    high, middle, low = split(local)
    mass = tile[6:7]
    alive = mass > 0.0
    exponent = jnp.where(alive, jnp.log2(jnp.where(alive, mass, 1.0)) + KAPPA * SOFTENING, NO_MASS)
    exponents = split(exponent)
    quadratic = three_rows(rows, 0, split(KAPPA * square)) + three_rows(rows, 3, split(KAPPA * mixed))
    quadratic = jnp.where(rows == 6, exponents[0], jnp.where(rows == 7, exponents[1], quadratic))
    ones = jnp.where(rows < 3, 1.0, jnp.where(rows == 3, exponents[2], 0.0))
    stacked = jnp.concatenate([high, high, high, middle, middle, low, quadratic, ones], axis=0)
    weights = split((mass * FORCE_SCALE) * jnp.where(rows < 3, local, jnp.where(rows == 3, 1.0, 0.0)))
    summed = jnp.concatenate([weights[0], weights[1], weights[2], jnp.zeros_like(local)], axis=0).astype(BF16)
    return stacked.T.astype(BF16), jnp.concatenate([summed, summed], axis=1)


def base_of_segment():
    return SPACING * lax.axis_index("curve").astype(F32)


def parity():
    return lax.rem(lax.axis_index("curve"), 2)


def list_blocks(table_ref, picks_ref, outer_ref, inner_ref):
    odd = parity()
    for h in range(HALO):
        outer_ref[h] = table_ref[picks_ref[0, odd * HALO + h]]
        inner_ref[h] = table_ref[picks_ref[0, (1 - odd) * HALO + h]]


def gather_kernel(
    x_hbm, v_hbm, m_hbm, counts_hbm, picks_hbm,
    table_ref, outer_ref, inner_ref,
    x_ref, v_ref, m_ref, flat_ref, counts_ref, picks_ref, sems,
):
    pairs = ((x_hbm, x_ref), (v_hbm, v_ref), (m_hbm, m_ref), (counts_hbm, counts_ref), (picks_hbm, picks_ref))
    copies = [pltpu.make_async_copy(source, target, sems.at[n]) for n, (source, target) in enumerate(pairs)]
    for copy in copies:
        copy.start()
    for copy in copies:
        copy.wait()
    for axis_id in range(3):
        flat_ref[pl.ds(axis_id, BLOCKS, stride=8), :] = x_ref[axis_id]
        flat_ref[pl.ds(3 + axis_id, BLOCKS, stride=8), :] = v_ref[axis_id]
    lane = lax.broadcasted_iota(jnp.int32, (1, LANES), 1)
    for b in range(BLOCKS):
        live = jnp.where(lane < counts_ref[0, b], m_ref[pl.ds(b, 1), :], 0.0)
        flat_ref[pl.ds(8 * b + 6, 1), :] = live
        flat_ref[pl.ds(8 * b + 7, 1), :] = jnp.zeros_like(live)
    for b in range(BLOCKS):
        table_ref[b] = flat_ref[pl.ds(8 * b, 8), :]
    list_blocks(table_ref, picks_ref, outer_ref, inner_ref)


def features_kernel(table_ref, *refs):
    target_ref, source_ref, sum_ref = refs[-3:]
    passed = (len(refs) - 3) // 2
    for n in range(passed):
        refs[passed + n][...] = refs[n][...]
    base = base_of_segment()
    rows = tile_rows()

    def own(b, carry):
        tile = table_ref[b]
        source_ref[b], sum_ref[b] = source_features(tile, base, rows)
        parts = target_features(tile, base, rows)
        for n in range(3):
            target_ref[b, :, n * LANES : (n + 1) * LANES] = parts[n]
        return carry

    lax.fori_loop(0, BLOCKS, own, 0, unroll=4)


def density_of(j, target_ref, source_ref, near_ref):
    right = target_ref[j, :, 2 * LANES : 3 * LANES]
    sources = [j] + [near_ref[n, 0, j] for n in range(NBR)]
    left = jnp.concatenate([source_ref[s] for s in sources], axis=0)
    weight = jnp.exp2(jnp.dot(left, right, preferred_element_type=F32))
    return BACKGROUND + jnp.sum(weight, axis=0, keepdims=True)


def listed_density_kernel(
    outer_ref, inner_ref, near_ref, picks_ref, target_ref, own_source_ref, own_sum_ref,
    outer_out_ref, inner_out_ref, source_ref, sum_ref,
):
    base = base_of_segment()
    odd = parity()
    rows = tile_rows()
    for b in range(BLOCKS):
        source_ref[b] = own_source_ref[b]
        sum_ref[b] = own_sum_ref[b]
    for h in range(HALO):
        for block_ref, side in ((outer_ref, odd), (inner_ref, 1 - odd)):
            at = BLOCKS + side * HALO + h
            source_ref[at], sum_ref[at] = source_features(block_ref[h], base, rows)

    for out_ref, side in ((outer_out_ref, odd), (inner_out_ref, 1 - odd)):
        for h in range(HALO):
            j = picks_ref[0, side * HALO + h]
            out_ref[pl.ds(h, 1), :] = density_of(j, target_ref, source_ref, near_ref)


def density_kernel(near_ref, target_ref, source_ref, rho_ref):
    def target(j, carry):
        rho_ref[j] = density_of(j, target_ref, source_ref, near_ref)
        return carry

    lax.fori_loop(0, BLOCKS, target, 0, unroll=16)


def advance(
    table_ref, rho_ref, outer_ref, inner_ref, near_ref, target_ref, source_ref, sum_ref, rho_of, inverse_of, done
):
    base = base_of_segment()
    rows = tile_rows()
    even = parity() == 0
    outer, inner = outer_ref[...], inner_ref[...]
    below = jnp.where(even, outer, inner)
    above = jnp.where(even, inner, outer)
    flat = [rho_ref[b] for b in range(BLOCKS)] + [below, above, jnp.ones((8, LANES), F32)]
    flat = jnp.concatenate(flat, axis=0)
    for s in range(CANDIDATES):
        column = jnp.broadcast_to(flat[s : s + 1, :], (LANES, LANES)).T
        rho_of[s] = column
        inverse_of[s] = 1.0 / column

    def target(j, carry):
        right = target_ref[j, :, 0 : 2 * LANES]
        mine = rho_ref[j]
        mine_inverse = 1.0 / mine
        sources = [j] + [near_ref[n, 0, j] for n in range(NBR)]
        wholes, lefts = [], []
        for s in sources:
            product = jnp.dot(source_ref[s], right, preferred_element_type=F32)
            distance = product[:, 0:LANES]
            approach = product[:, LANES : 2 * LANES]
            closing = jnp.minimum(approach, 0.0) / (distance * (mine + rho_of[s]))
            factor = jnp.exp2(distance) * (closing + (mine_inverse + inverse_of[s]))
            high = factor.astype(BF16)
            low = (factor - high.astype(F32)).astype(BF16)
            wholes += [high, low]
            lefts.append(sum_ref[s])
        total = jnp.dot(jnp.concatenate(lefts, axis=1), jnp.concatenate(wholes, axis=0), preferred_element_type=F32)
        sums = total[0:8] + total[8:16] + total[16:24]
        tile = table_ref[j]
        local = local_tile(tile, base, rows)
        accel = jnp.where(rows < 3, local * sums[3:4] - sums, 0.0)
        kicked = tile + TIME_STEP * pltpu.roll(accel, 3, axis=0)
        drift = pltpu.roll(kicked, 5, axis=0)
        done(j, jnp.where(rows < 3, kicked + TIME_STEP * drift, kicked))
        return carry

    lax.fori_loop(0, BLOCKS, target, 0, unroll=16)


def force_move_kernel(
    table_ref, rho_ref, outer_ref, inner_ref, near_ref, target_ref, source_ref, sum_ref, slot_hbm,
    stay_ref, send_ref, rho_of, inverse_of, filled, slot_ref, sem, moved_ref,
):
    copy = pltpu.make_async_copy(slot_hbm, slot_ref, sem)
    copy.start()
    me = lax.axis_index("group")
    rows = tile_rows()
    groups = send_ref.shape[0]
    for g in range(groups):
        filled[g] = 0
        for k in range(MOVES):
            send_ref[g, k] = jnp.full((8, LANES), -1.0, F32)
    for b in range(BLOCKS):
        stay_ref[b] = jnp.zeros((8, LANES), F32)
    copy.wait()

    def done(b, tile):
        moved_ref[b] = tile

    advance(
        table_ref, rho_ref, outer_ref, inner_ref, near_ref, target_ref, source_ref, sum_ref, rho_of, inverse_of, done
    )

    def route(b, carry):
        owner = slot_ref[0, b] // BLOCKS
        slot = slot_ref[0, b] % BLOCKS
        tagged = jnp.where(rows == 7, jnp.full((8, LANES), slot, jnp.int32).astype(F32), moved_ref[b])

        @pl.when(owner == me)
        def _():
            stay_ref[slot] = tagged

        @pl.when(owner != me)
        def _():
            place = jnp.minimum(filled[owner], MOVES - 1)
            send_ref[owner, place] = tagged
            filled[owner] = place + 1

        return carry

    lax.fori_loop(0, BLOCKS, route, 0)


def arrive_kernel(stay_ref, arrived_ref, picks_hbm, table_ref, outer_ref, inner_ref, picks_ref, sem):
    copy = pltpu.make_async_copy(picks_hbm, picks_ref, sem)
    copy.start()
    groups = arrived_ref.shape[0]
    tiles = [arrived_ref[g, k] for g in range(groups) for k in range(MOVES)]
    tags = [jnp.broadcast_to(tile[7:8], (8, LANES)) for tile in tiles]
    for s in range(BLOCKS):
        value = stay_ref[s]
        for tile, tag in zip(tiles, tags):
            value = jnp.where(tag == float(s), tile, value)
        table_ref[s] = value
    copy.wait()
    list_blocks(table_ref, picks_ref, outer_ref, inner_ref)


def force_out_kernel(
    table_ref, rho_ref, outer_ref, inner_ref, near_ref, target_ref, source_ref, sum_ref,
    x_ref, v_ref, rho_out_ref, rho_of, inverse_of, flat_ref,
):
    def done(b, tile):
        flat_ref[pl.ds(pl.multiple_of(8 * b, 8), 8), :] = tile

    advance(
        table_ref, rho_ref, outer_ref, inner_ref, near_ref, target_ref, source_ref, sum_ref, rho_of, inverse_of, done
    )
    for b in range(BLOCKS):
        rho_out_ref[pl.ds(b, 1), :] = rho_ref[b]
    for axis_id in range(3):
        x_ref[axis_id] = flat_ref[pl.ds(axis_id, BLOCKS, stride=8), :]
        v_ref[axis_id] = flat_ref[pl.ds(3 + axis_id, BLOCKS, stride=8), :]


def shape(*dims, dtype=F32):
    return jax.ShapeDtypeStruct(dims, dtype)


TABLE = shape(BLOCKS, 8, LANES)
LISTED = shape(HALO, 8, LANES)


def call(kernel, out_shape, in_specs, scratch=(), flops=0, grant=16 << 20):
    return pl.pallas_call(
        kernel,
        out_shape=out_shape,
        in_specs=in_specs,
        out_specs=[VMEM] * len(out_shape),
        scratch_shapes=list(scratch),
        cost_estimate=pl.CostEstimate(flops=flops, bytes_accessed=200000, transcendentals=0),
        compiler_params=pltpu.CompilerParams(vmem_limit_bytes=grant),
    )


def swap_outer(item):
    count = lax.axis_size("curve")
    pairs = [(i, (i + 1) % count) for i in range(1, count, 2)]
    return lax.ppermute(item, "curve", pairs + [(target, source) for source, target in pairs])


def swap_inner(item):
    pairs = [(i, i + 1) for i in range(0, lax.axis_size("curve"), 2)]
    return lax.ppermute(item, "curve", pairs + [(target, source) for source, target in pairs])


SOURCES = (
    shape(CANDIDATES, LANES, FEATURES, dtype=BF16),
    shape(CANDIDATES, 32, 2 * LANES, dtype=BF16),
)
OWN_SOURCES = (
    shape(BLOCKS, LANES, FEATURES, dtype=BF16),
    shape(BLOCKS, 32, 2 * LANES, dtype=BF16),
)


def half_step(table, outer, inner, near, picks, passed=()):
    outer = swap_outer(outer)
    inner = swap_inner(inner)
    passed = (near, picks) + tuple(passed)
    near, picks, *passed, targets, own_source, own_sum = call(
        features_kernel,
        tuple(shape(*item.shape, dtype=item.dtype) for item in passed)
        + (shape(BLOCKS, FEATURES, 3 * LANES, dtype=BF16),)
        + OWN_SOURCES,
        [VMEM] * (1 + len(passed)),
    )(table, *passed)
    outer_rho, inner_rho, sources, sums = call(
        listed_density_kernel,
        (shape(HALO, LANES), shape(HALO, LANES)) + SOURCES,
        [VMEM, VMEM, SMEM, SMEM, VMEM, VMEM, VMEM],
    )(outer, inner, near, picks, targets, own_source, own_sum)
    outer_rho = swap_outer(outer_rho)
    inner_rho = swap_inner(inner_rho)
    (rho,) = call(density_kernel, (shape(BLOCKS, 1, LANES),), [SMEM, VMEM, VMEM])(near, targets, sources)
    return (table, rho, outer_rho, inner_rho, near, targets, sources, sums), passed


FORCE_SPECS = [VMEM, VMEM, VMEM, VMEM, SMEM, VMEM, VMEM, VMEM]
FORCE_SCRATCH = [pltpu.VMEM((CANDIDATES, LANES, LANES), F32)] * 2


def body(x, v, masses, counts, near_first, picks_first, new_slot, near_second, picks_second):
    groups = lax.axis_size("group")
    near_first = jnp.transpose(near_first, (2, 0, 1))
    near_second = jnp.transpose(near_second, (2, 0, 1))
    table, outer, inner = call(
        gather_kernel,
        (TABLE, LISTED, LISTED),
        [HBM] * 5,
        [
            pltpu.VMEM((3, BLOCKS, LANES), F32),
            pltpu.VMEM((3, BLOCKS, LANES), F32),
            pltpu.VMEM((BLOCKS, LANES), F32),
            pltpu.VMEM((8 * BLOCKS, LANES), F32),
            pltpu.SMEM((1, BLOCKS), jnp.int32),
            pltpu.SMEM((1, 2 * HALO), jnp.int32),
            pltpu.SemaphoreType.DMA((5,)),
        ],
        grant=GATHER_GRANT,
    )(jnp.transpose(x[0], (1, 0, 2)), jnp.transpose(v[0], (1, 0, 2)), masses[0], counts, picks_first)
    state, (new_slot, picks_second) = half_step(table, outer, inner, near_first, picks_first, (new_slot, picks_second))
    stay, send = call(
        force_move_kernel,
        (TABLE, shape(groups, MOVES, 8, LANES)),
        FORCE_SPECS + [HBM],
        FORCE_SCRATCH
        + [pltpu.SMEM((groups,), jnp.int32), pltpu.SMEM((1, BLOCKS), jnp.int32), pltpu.SemaphoreType.DMA]
        + [pltpu.VMEM((BLOCKS, 8, LANES), F32)],
    )(*state, new_slot)
    arrived = lax.all_to_all(send, "group", 0, 0)
    table, outer, inner = call(
        arrive_kernel,
        (TABLE, LISTED, LISTED),
        [VMEM, VMEM, HBM],
        [pltpu.SMEM((1, 2 * HALO), jnp.int32), pltpu.SemaphoreType.DMA],
    )(stay, arrived, picks_second)
    state, _ = half_step(table, outer, inner, near_second, picks_second)
    x_out, v_out, rho = call(
        force_out_kernel,
        (shape(3, BLOCKS, LANES), shape(3, BLOCKS, LANES), shape(BLOCKS, LANES)),
        FORCE_SPECS,
        FORCE_SCRATCH + [pltpu.VMEM((8 * BLOCKS, LANES), F32)],
    )(*state)
    return jnp.transpose(x_out, (1, 0, 2))[None], jnp.transpose(v_out, (1, 0, 2))[None], rho[None]


def solution(mesh):
    in_specs = (
        P("group", "curve", None, None),
        P("group", "curve", None, None),
        P("group", "curve", None),
        P("group", "curve"),
        P("group", "curve", None),
        P("group", "curve"),
        P("group", "curve"),
        P("group", "curve", None),
        P("group", "curve"),
    )
    out_specs = (
        P("group", "curve", None, None),
        P("group", "curve", None, None),
        P("group", "curve", None),
    )
    return jax.shard_map(body, mesh=mesh, in_specs=in_specs, out_specs=out_specs, check_vma=False)
```

```python
import math

import jax
import jax.numpy as jnp
from jax import lax
from jax.experimental import pallas as pl
from jax.experimental.pallas import tpu as pltpu
from jax.sharding import PartitionSpec as P


SOFTENING = 0.0025
BACKGROUND = 0.5
TIME_STEP = 0.1
SPACING = 0.6

BLOCKS = 16
HALO = 4
NBR = 6
CANDIDATES = BLOCKS + 2 * HALO
LANES = 128
FEATURES = 64
MOVES = 2
GATHER_GRANT = 63_000_000
KAPPA = 4.0 * math.log2(math.e)
MASS_SCALE = 2.0 ** (KAPPA * SOFTENING)
FORCE_SCALE = 8.0 * MASS_SCALE
NO_MASS = -4096.0

F32 = jnp.float32
BF16 = jnp.bfloat16
VMEM = pl.BlockSpec(memory_space=pltpu.VMEM)
SMEM = pl.BlockSpec(memory_space=pltpu.SMEM)
HBM = pl.BlockSpec(memory_space=pltpu.HBM)


def rounded(value):
    return value.astype(BF16).astype(F32)


def split(value):
    high = rounded(value)
    rest = value - high
    middle = rounded(rest)
    return high, middle, rest - middle


def tile_rows():
    return lax.broadcasted_iota(jnp.int32, (8, LANES), 0)


def three_rows(rows, first, parts):
    return jnp.where(
        rows == first, parts[0], jnp.where(rows == first + 1, parts[1], jnp.where(rows == first + 2, parts[2], 0.0))
    )


def local_tile(tile, base, rows):
    shifted = jnp.where(rows == 0, tile - base, tile)
    return jnp.where(rows < 6, shifted, 0.0)


def swapped(local, rows):
    down = pltpu.roll(local, 5, axis=0)
    up = pltpu.roll(local, 3, axis=0)
    return jnp.where(rows < 3, down, jnp.where(rows < 6, up, 0.0))


def quadratics(local, other, rows):
    square = jnp.sum(jnp.where(rows < 3, local * local, 0.0), axis=0, keepdims=True)
    mixed = jnp.sum(jnp.where(rows < 3, local * other, 0.0), axis=0, keepdims=True)
    return square, mixed


def target_features(tile, base, rows):
    local = local_tile(tile, base, rows)
    other = swapped(local, rows)
    square, mixed = quadratics(local, other, rows)
    near = split(jnp.where(rows < 3, (2.0 * KAPPA) * local, 0.0))
    flow = split(-KAPPA * other)
    minus = jnp.where(rows < 3, -1.0, 0.0)
    plus = jnp.where((rows >= 3) & (rows < 6), 1.0, 0.0)
    last_near = three_rows(rows, 0, split(-KAPPA * (square + SOFTENING)))
    last_flow = three_rows(rows, 0, split(KAPPA * mixed))
    near = [near[0], near[1], near[2], near[0], near[1], near[0]]
    flow = [flow[0], flow[1], flow[2], flow[0], flow[1], flow[0]]
    distance = jnp.concatenate(near + [minus, last_near], axis=0)
    approach = jnp.concatenate(flow + [plus, last_flow], axis=0)
    weighted = jnp.concatenate(
        near + [jnp.where(rows >= 6, 1.0, minus), jnp.where(rows == 3, 1.0, last_near)], axis=0
    )
    return distance.astype(BF16), approach.astype(BF16), weighted.astype(BF16)


def source_features(tile, base, rows):
    local = local_tile(tile, base, rows)
    other = swapped(local, rows)
    square, mixed = quadratics(local, other, rows)
    high, middle, low = split(local)
    mass = tile[6:7]
    alive = mass > 0.0
    exponent = jnp.where(alive, jnp.log2(jnp.where(alive, mass, 1.0)) + KAPPA * SOFTENING, NO_MASS)
    exponents = split(exponent)
    quadratic = three_rows(rows, 0, split(KAPPA * square)) + three_rows(rows, 3, split(KAPPA * mixed))
    quadratic = jnp.where(rows == 6, exponents[0], jnp.where(rows == 7, exponents[1], quadratic))
    ones = jnp.where(rows < 3, 1.0, jnp.where(rows == 3, exponents[2], 0.0))
    stacked = jnp.concatenate([high, high, high, middle, middle, low, quadratic, ones], axis=0)
    weights = split((mass * FORCE_SCALE) * jnp.where(rows < 3, local, jnp.where(rows == 3, 1.0, 0.0)))
    summed = jnp.concatenate([weights[0], weights[1], weights[2], jnp.zeros_like(local)], axis=0).astype(BF16)
    return stacked.T.astype(BF16), summed


def base_of_segment():
    return SPACING * lax.axis_index("curve").astype(F32)


def parity():
    return lax.rem(lax.axis_index("curve"), 2)


def list_blocks(table_ref, picks_ref, outer_ref, inner_ref):
    odd = parity()
    for h in range(HALO):
        outer_ref[h] = table_ref[picks_ref[0, odd * HALO + h]]
        inner_ref[h] = table_ref[picks_ref[0, (1 - odd) * HALO + h]]


def gather_kernel(
    x_hbm, v_hbm, m_hbm, counts_hbm, picks_hbm,
    table_ref, outer_ref, inner_ref,
    x_ref, v_ref, m_ref, flat_ref, counts_ref, picks_ref, sems,
):
    pairs = ((x_hbm, x_ref), (v_hbm, v_ref), (m_hbm, m_ref), (counts_hbm, counts_ref), (picks_hbm, picks_ref))
    copies = [pltpu.make_async_copy(source, target, sems.at[n]) for n, (source, target) in enumerate(pairs)]
    for copy in copies:
        copy.start()
    for copy in copies:
        copy.wait()
    for axis_id in range(3):
        flat_ref[pl.ds(axis_id, BLOCKS, stride=8), :] = x_ref[axis_id]
        flat_ref[pl.ds(3 + axis_id, BLOCKS, stride=8), :] = v_ref[axis_id]
    lane = lax.broadcasted_iota(jnp.int32, (1, LANES), 1)
    for b in range(BLOCKS):
        live = jnp.where(lane < counts_ref[0, b], m_ref[pl.ds(b, 1), :], 0.0)
        flat_ref[pl.ds(8 * b + 6, 1), :] = live
        flat_ref[pl.ds(8 * b + 7, 1), :] = jnp.zeros_like(live)
    for b in range(BLOCKS):
        table_ref[b] = flat_ref[pl.ds(8 * b, 8), :]
    list_blocks(table_ref, picks_ref, outer_ref, inner_ref)


def features_kernel(table_ref, *refs):
    target_ref, source_ref, sum_ref = refs[-3:]
    passed = (len(refs) - 3) // 2
    for n in range(passed):
        refs[passed + n][...] = refs[n][...]
    base = base_of_segment()
    rows = tile_rows()

    def own(b, carry):
        tile = table_ref[b]
        source_ref[b], sum_ref[b] = source_features(tile, base, rows)
        parts = target_features(tile, base, rows)
        for n in range(3):
            target_ref[b, :, n * LANES : (n + 1) * LANES] = parts[n]
        return carry

    lax.fori_loop(0, BLOCKS, own, 0, unroll=4)


def density_of(j, target_ref, source_ref, near_ref):
    right = target_ref[j, :, 2 * LANES : 3 * LANES]
    sources = [j] + [near_ref[n, 0, j] for n in range(NBR)]
    left = jnp.concatenate([source_ref[s] for s in sources], axis=0)
    weight = jnp.exp2(jnp.dot(left, right, preferred_element_type=F32))
    return BACKGROUND + jnp.sum(weight, axis=0, keepdims=True)


def listed_density_kernel(
    outer_ref, inner_ref, near_ref, picks_ref, target_ref, own_source_ref, own_sum_ref,
    outer_out_ref, inner_out_ref, source_ref, sum_ref,
):
    base = base_of_segment()
    odd = parity()
    rows = tile_rows()
    for b in range(BLOCKS):
        source_ref[b] = own_source_ref[b]
        sum_ref[b] = own_sum_ref[b]
    for h in range(HALO):
        for block_ref, side in ((outer_ref, odd), (inner_ref, 1 - odd)):
            at = BLOCKS + side * HALO + h
            source_ref[at], sum_ref[at] = source_features(block_ref[h], base, rows)

    for out_ref, side in ((outer_out_ref, odd), (inner_out_ref, 1 - odd)):
        for h in range(HALO):
            j = picks_ref[0, side * HALO + h]
            out_ref[pl.ds(h, 1), :] = density_of(j, target_ref, source_ref, near_ref)


def density_kernel(near_ref, target_ref, source_ref, rho_ref):
    def target(j, carry):
        rho_ref[j] = density_of(j, target_ref, source_ref, near_ref)
        return carry

    lax.fori_loop(0, BLOCKS, target, 0, unroll=16)


def advance(
    table_ref, rho_ref, outer_ref, inner_ref, near_ref, target_ref, source_ref, sum_ref, rho_of, inverse_of, done
):
    base = base_of_segment()
    rows = tile_rows()
    even = parity() == 0
    outer, inner = outer_ref[...], inner_ref[...]
    below = jnp.where(even, outer, inner)
    above = jnp.where(even, inner, outer)
    flat = [rho_ref[b] for b in range(BLOCKS)] + [below, above, jnp.ones((8, LANES), F32)]
    flat = jnp.concatenate(flat, axis=0)
    for s in range(CANDIDATES):
        column = jnp.broadcast_to(flat[s : s + 1, :], (LANES, LANES)).T
        rho_of[s] = column
        inverse_of[s] = 1.0 / column

    def target(j, carry):
        right = target_ref[j, :, 0 : 2 * LANES]
        mine = rho_ref[j]
        mine_inverse = 1.0 / mine
        sources = [j] + [near_ref[n, 0, j] for n in range(NBR)]
        wholes, lefts = [], []
        for s in sources:
            product = jnp.dot(source_ref[s], right, preferred_element_type=F32)
            distance = product[:, 0:LANES]
            approach = product[:, LANES : 2 * LANES]
            closing = jnp.minimum(approach, 0.0) / (distance * (mine + rho_of[s]))
            factor = jnp.exp2(distance) * (closing + (mine_inverse + inverse_of[s]))
            high = factor.astype(BF16)
            low = (factor - high.astype(F32)).astype(BF16)
            wholes.append(jnp.concatenate([high, low], axis=1))
            lefts.append(sum_ref[s])
        total = jnp.dot(jnp.concatenate(lefts, axis=1), jnp.concatenate(wholes, axis=0), preferred_element_type=F32)
        total = total[:, 0:LANES] + total[:, LANES : 2 * LANES]
        sums = total[0:8] + total[8:16] + total[16:24]
        tile = table_ref[j]
        local = local_tile(tile, base, rows)
        accel = jnp.where(rows < 3, local * sums[3:4] - sums, 0.0)
        kicked = tile + TIME_STEP * pltpu.roll(accel, 3, axis=0)
        drift = pltpu.roll(kicked, 5, axis=0)
        done(j, jnp.where(rows < 3, kicked + TIME_STEP * drift, kicked))
        return carry

    lax.fori_loop(0, BLOCKS, target, 0, unroll=16)


def force_move_kernel(
    table_ref, rho_ref, outer_ref, inner_ref, near_ref, target_ref, source_ref, sum_ref, slot_hbm,
    stay_ref, send_ref, rho_of, inverse_of, filled, slot_ref, sem, moved_ref,
):
    copy = pltpu.make_async_copy(slot_hbm, slot_ref, sem)
    copy.start()
    me = lax.axis_index("group")
    rows = tile_rows()
    groups = send_ref.shape[0]
    for g in range(groups):
        filled[g] = 0
        for k in range(MOVES):
            send_ref[g, k] = jnp.full((8, LANES), -1.0, F32)
    for b in range(BLOCKS):
        stay_ref[b] = jnp.zeros((8, LANES), F32)
    copy.wait()

    def done(b, tile):
        moved_ref[b] = tile

    advance(
        table_ref, rho_ref, outer_ref, inner_ref, near_ref, target_ref, source_ref, sum_ref, rho_of, inverse_of, done
    )

    def route(b, carry):
        owner = slot_ref[0, b] // BLOCKS
        slot = slot_ref[0, b] % BLOCKS
        tagged = jnp.where(rows == 7, jnp.full((8, LANES), slot, jnp.int32).astype(F32), moved_ref[b])

        @pl.when(owner == me)
        def _():
            stay_ref[slot] = tagged

        @pl.when(owner != me)
        def _():
            place = jnp.minimum(filled[owner], MOVES - 1)
            send_ref[owner, place] = tagged
            filled[owner] = place + 1

        return carry

    lax.fori_loop(0, BLOCKS, route, 0)


def arrive_kernel(stay_ref, arrived_ref, picks_hbm, table_ref, outer_ref, inner_ref, picks_ref, sem):
    copy = pltpu.make_async_copy(picks_hbm, picks_ref, sem)
    copy.start()
    groups = arrived_ref.shape[0]
    tiles = [arrived_ref[g, k] for g in range(groups) for k in range(MOVES)]
    tags = [jnp.broadcast_to(tile[7:8], (8, LANES)) for tile in tiles]
    for s in range(BLOCKS):
        value = stay_ref[s]
        for tile, tag in zip(tiles, tags):
            value = jnp.where(tag == float(s), tile, value)
        table_ref[s] = value
    copy.wait()
    list_blocks(table_ref, picks_ref, outer_ref, inner_ref)


def force_out_kernel(
    table_ref, rho_ref, outer_ref, inner_ref, near_ref, target_ref, source_ref, sum_ref,
    x_ref, v_ref, rho_out_ref, rho_of, inverse_of, flat_ref,
):
    def done(b, tile):
        flat_ref[pl.ds(pl.multiple_of(8 * b, 8), 8), :] = tile

    advance(
        table_ref, rho_ref, outer_ref, inner_ref, near_ref, target_ref, source_ref, sum_ref, rho_of, inverse_of, done
    )
    for b in range(BLOCKS):
        rho_out_ref[pl.ds(b, 1), :] = rho_ref[b]
    for axis_id in range(3):
        x_ref[axis_id] = flat_ref[pl.ds(axis_id, BLOCKS, stride=8), :]
        v_ref[axis_id] = flat_ref[pl.ds(3 + axis_id, BLOCKS, stride=8), :]


def shape(*dims, dtype=F32):
    return jax.ShapeDtypeStruct(dims, dtype)


TABLE = shape(BLOCKS, 8, LANES)
LISTED = shape(HALO, 8, LANES)


def call(kernel, out_shape, in_specs, scratch=(), flops=0, grant=16 << 20):
    return pl.pallas_call(
        kernel,
        out_shape=out_shape,
        in_specs=in_specs,
        out_specs=[VMEM] * len(out_shape),
        scratch_shapes=list(scratch),
        cost_estimate=pl.CostEstimate(flops=flops, bytes_accessed=200000, transcendentals=0),
        compiler_params=pltpu.CompilerParams(vmem_limit_bytes=grant),
    )


def swap_outer(item):
    count = lax.axis_size("curve")
    pairs = [(i, (i + 1) % count) for i in range(1, count, 2)]
    return lax.ppermute(item, "curve", pairs + [(target, source) for source, target in pairs])


def swap_inner(item):
    pairs = [(i, i + 1) for i in range(0, lax.axis_size("curve"), 2)]
    return lax.ppermute(item, "curve", pairs + [(target, source) for source, target in pairs])


SOURCES = (
    shape(CANDIDATES, LANES, FEATURES, dtype=BF16),
    shape(CANDIDATES, 32, LANES, dtype=BF16),
)
OWN_SOURCES = (
    shape(BLOCKS, LANES, FEATURES, dtype=BF16),
    shape(BLOCKS, 32, LANES, dtype=BF16),
)


def half_step(table, outer, inner, near, picks, passed=()):
    outer = swap_outer(outer)
    inner = swap_inner(inner)
    passed = (near, picks) + tuple(passed)
    near, picks, *passed, targets, own_source, own_sum = call(
        features_kernel,
        tuple(shape(*item.shape, dtype=item.dtype) for item in passed)
        + (shape(BLOCKS, FEATURES, 3 * LANES, dtype=BF16),)
        + OWN_SOURCES,
        [VMEM] * (1 + len(passed)),
    )(table, *passed)
    outer_rho, inner_rho, sources, sums = call(
        listed_density_kernel,
        (shape(HALO, LANES), shape(HALO, LANES)) + SOURCES,
        [VMEM, VMEM, SMEM, SMEM, VMEM, VMEM, VMEM],
    )(outer, inner, near, picks, targets, own_source, own_sum)
    outer_rho = swap_outer(outer_rho)
    inner_rho = swap_inner(inner_rho)
    (rho,) = call(density_kernel, (shape(BLOCKS, 1, LANES),), [SMEM, VMEM, VMEM])(near, targets, sources)
    return (table, rho, outer_rho, inner_rho, near, targets, sources, sums), passed


FORCE_SPECS = [VMEM, VMEM, VMEM, VMEM, SMEM, VMEM, VMEM, VMEM]
FORCE_SCRATCH = [pltpu.VMEM((CANDIDATES, LANES, LANES), F32)] * 2


def body(x, v, masses, counts, near_first, picks_first, new_slot, near_second, picks_second):
    groups = lax.axis_size("group")
    near_first = jnp.transpose(near_first, (2, 0, 1))
    near_second = jnp.transpose(near_second, (2, 0, 1))
    table, outer, inner = call(
        gather_kernel,
        (TABLE, LISTED, LISTED),
        [HBM] * 5,
        [
            pltpu.VMEM((3, BLOCKS, LANES), F32),
            pltpu.VMEM((3, BLOCKS, LANES), F32),
            pltpu.VMEM((BLOCKS, LANES), F32),
            pltpu.VMEM((8 * BLOCKS, LANES), F32),
            pltpu.SMEM((1, BLOCKS), jnp.int32),
            pltpu.SMEM((1, 2 * HALO), jnp.int32),
            pltpu.SemaphoreType.DMA((5,)),
        ],
        grant=GATHER_GRANT,
    )(jnp.transpose(x[0], (1, 0, 2)), jnp.transpose(v[0], (1, 0, 2)), masses[0], counts, picks_first)
    state, (new_slot, picks_second) = half_step(table, outer, inner, near_first, picks_first, (new_slot, picks_second))
    stay, send = call(
        force_move_kernel,
        (TABLE, shape(groups, MOVES, 8, LANES)),
        FORCE_SPECS + [HBM],
        FORCE_SCRATCH
        + [pltpu.SMEM((groups,), jnp.int32), pltpu.SMEM((1, BLOCKS), jnp.int32), pltpu.SemaphoreType.DMA]
        + [pltpu.VMEM((BLOCKS, 8, LANES), F32)],
    )(*state, new_slot)
    arrived = lax.all_to_all(send, "group", 0, 0)
    table, outer, inner = call(
        arrive_kernel,
        (TABLE, LISTED, LISTED),
        [VMEM, VMEM, HBM],
        [pltpu.SMEM((1, 2 * HALO), jnp.int32), pltpu.SemaphoreType.DMA],
    )(stay, arrived, picks_second)
    state, _ = half_step(table, outer, inner, near_second, picks_second)
    x_out, v_out, rho = call(
        force_out_kernel,
        (shape(3, BLOCKS, LANES), shape(3, BLOCKS, LANES), shape(BLOCKS, LANES)),
        FORCE_SPECS,
        FORCE_SCRATCH + [pltpu.VMEM((8 * BLOCKS, LANES), F32)],
    )(*state)
    return jnp.transpose(x_out, (1, 0, 2))[None], jnp.transpose(v_out, (1, 0, 2))[None], rho[None]


def solution(mesh):
    in_specs = (
        P("group", "curve", None, None),
        P("group", "curve", None, None),
        P("group", "curve", None),
        P("group", "curve"),
        P("group", "curve", None),
        P("group", "curve"),
        P("group", "curve"),
        P("group", "curve", None),
        P("group", "curve"),
    )
    out_specs = (
        P("group", "curve", None, None),
        P("group", "curve", None, None),
        P("group", "curve", None),
    )
    return jax.shard_map(body, mesh=mesh, in_specs=in_specs, out_specs=out_specs, check_vma=False)
```
